512 devices in a mesh: region: 128 (over z, x, core), pair: 4 (over y).
Axes of the slice: x: 4, y: 4, z: 16, core: 2. Of those that a mesh axis runs over, the one named last changes fastest.
Arguments:
- phi: bfloat16 [1024, 128, 32, 128], P('region', None, 'pair'), may hold values from -0.09375 to 0.09375
- potential: float32 [128, 32, 128], P('region', 'pair'), may hold values from -2 to 2
- pair_list: int32 [32, 2], replicated, may hold values from 0 to 7, as said below
- support: int32 [8, 128], replicated, may hold values 0 or 1
Outputs:
- intersection: float32 [32, 16384], P('pair', 'region')
- hamiltonian: float32 [32, 16384], P('pair', 'region')
- hphi: bfloat16 [1024, 128, 32, 128], P('region', None, 'pair')
The draws below stay inside these ranges and needn't reach their ends.
Inputs may be any that keep to these rules, and one draw needn't show every extreme that they name: `pair_list`: each row is an ordered pair of block numbers; no pair appears twice.
All inputs are finite; a program needn't handle non-finite values.
Results may differ from the reference program's by a relative error of at most 0.0029.
Values may be sent and summed in bfloat16 or wider, within the bound.
No kernel may reach another device: no remote copies, remote signals or barrier semaphores. Data moves between devices by JAX's collectives and lax.ppermute only.
A program may use at most 64 MiB of HBM per device.

```python
import jax
import jax.numpy as jnp
from jax import lax

W = 128
NBLK = 8
PLANES = 1
PY = 32
PZ = 128
M = 1024
X = 128
NPAIRS = 32
N_REGION = 128


def draw_pair_list(key, part):
    key_order, key_slot = jax.random.split(key)
    order = jax.random.permutation(key_order, NBLK * NBLK)
    target = (NBLK - 1) * NBLK
    slot = jax.random.randint(key_slot, (), 0, NPAIRS)
    order = jnp.where(order == target, order[slot], order)
    order = order.at[slot].set(target)
    chosen = order[:NPAIRS]
    return jnp.stack([chosen // NBLK, chosen % NBLK], axis=1).astype(jnp.int32)


def with_ends(array, stream_key, least, largest):
    dims = array.shape
    spot = [jax.random.randint(jax.random.fold_in(stream_key, axis), (), 0, dims[axis]) for axis in range(len(dims))]
    array = array.at[tuple(spot)].set(least)
    longest = dims.index(max(dims))
    spot[longest] = (spot[longest] + 1) % dims[longest]
    return array.at[tuple(spot)].set(largest)


def levels(own_key, extent, pieces, least, largest):
    loudness, own = 1.0, jax.random.fold_in(own_key, 6)
    for position, blocks in pieces:
        heights = jnp.exp(jax.random.uniform(jax.random.fold_in(own, position), (blocks,), jnp.float32, least / len(pieces), largest / len(pieces)))
        loudness = loudness * jnp.repeat(heights, extent[position] // blocks).reshape([-1 if axis == position else 1 for axis in range(len(extent))])
    return loudness


def normal_values(own_key, shape, scale, bound, cuts=(), held_as=jnp.bfloat16):
    array = jax.random.normal(own_key, shape, jnp.float32) * scale
    if len(cuts) > 0:
        array = levels(own_key, shape, cuts, -0.22, 0.18) * array
    return jnp.clip(array, min=-bound, max=bound).astype(held_as)


def setup_inputs(seed: int = 0) -> dict:
    arg_keys = jax.random.split(jax.random.key(seed), 5)
    return {
        "phi": normal_values(arg_keys[0], (M, X, PY, PZ), (X * PY) ** -0.5, 0.09375, ((0, 128), (2, 4))),
        "potential": jnp.clip(jax.random.uniform(arg_keys[1], (X, PY, PZ), jnp.float32, -2.0, 2.0) * levels(arg_keys[1], (X, PY, PZ), ((0, 128), (1, 4)), -0.4, 0.0), -2.0, 2.0),
        "pair_list": draw_pair_list(jax.random.fold_in(arg_keys[4], 71), 0),
        "support": with_ends((jax.random.randint(arg_keys[3], (NBLK, N_REGION), 0, 2) < 1).astype(jnp.int32), jax.random.fold_in(arg_keys[3], 1), 0, 1),
    }


def apply_block(values_low, potential, keep_mask):
    values = values_low.astype(jnp.float32)
    laplace_sum = jnp.roll(values, -1, axis=1) + jnp.roll(values, 1, axis=1) - 6.0 * values
    laplace_sum = laplace_sum + jnp.roll(values, -1, axis=2) + jnp.roll(values, 1, axis=2)
    z_padded = jnp.pad(values, ((0, 0), (0, 0), (0, 0), (1, 1)))
    laplace_sum = laplace_sum + z_padded[..., 2:] + z_padded[..., :-2]
    applied = (-0.5 * laplace_sum + potential[None] * values) * keep_mask[:, :, None, None]
    return applied.astype(jnp.bfloat16)


def reference(phi, potential, pair_list, support):
    live_mask = jnp.repeat(jnp.repeat(support, W, axis=0), PLANES, axis=1)
    confined = jnp.where(live_mask[:, :, None, None] > 0, phi, jnp.zeros_like(phi))
    keep_mask = live_mask.astype(jnp.float32)
    applied = lax.map(lambda members: apply_block(members[0], potential, members[1]),
                      (confined.reshape(NBLK, W, X, PY, PZ), keep_mask.reshape(NBLK, W, X)))
    applied = applied.reshape(M, X, PY, PZ)
    flat_data = confined.reshape(M, X * PY * PZ)
    flat_applied = applied.reshape(M, X * PY * PZ)
    contract_dims = (((1,), (1,)), ((), ()))

    def pair_terms(pair_row):
        first_row = (pair_row[0] * W).astype(jnp.int32)
        second_row = (pair_row[1] * W).astype(jnp.int32)
        left_rows = lax.dynamic_slice_in_dim(flat_data, first_row, W, 0)
        right_rows = lax.dynamic_slice_in_dim(flat_data, second_row, W, 0)
        ham_rows = lax.dynamic_slice_in_dim(flat_applied, second_row, W, 0)
        return (lax.dot_general(left_rows, right_rows, contract_dims, preferred_element_type=jnp.float32),
                lax.dot_general(left_rows, ham_rows, contract_dims, preferred_element_type=jnp.float32))

    intersection, hamiltonian = lax.map(pair_terms, pair_list)
    return intersection.reshape(NPAIRS, W * W), hamiltonian.reshape(NPAIRS, W * W), applied
```

```python
import functools

import jax
import jax.numpy as jnp
from jax import lax
from jax.experimental import pallas as pl
from jax.experimental.pallas import tpu as pltpu
from jax.sharding import Mesh, PartitionSpec as P

W = 128
NB = 8
ROWS = 8
DEPTH = 128
PLANES = 128
PAIRS = 32
ZD, XD, CD, YD = 16, 4, 2, 4
REGION = ("z", "x", "c")
F32 = jnp.float32
BF16 = jnp.bfloat16


def flag(support, block, plane):
    return (support[block * PLANES + plane] > 0).astype(F32)


def lane_neighbours(tile, lane):
    axis = tile.ndim - 1
    low = jnp.where(lane == 0, 0.0, pltpu.roll(tile, 1, axis))
    high = jnp.where(lane == DEPTH - 1, 0.0, pltpu.roll(tile, DEPTH - 1, axis))
    return low + high


def region_kernel(pairs, support, where, own, ahead, behind, below, above, pot,
                  mine, theirs, right, near, tmp_s, tmp_h):
    plane, core = where[0], where[1]
    nxt = lax.rem(plane + 1, PLANES)
    prv = lax.rem(plane + PLANES - 1, PLANES)
    lane = lax.broadcasted_iota(jnp.int32, (64, DEPTH), 1)

    @pl.loop(0, NB)
    def _(block):
        live_next = flag(support, block, nxt)
        live_prev = flag(support, block, prv)
        for y in range(ROWS):
            cols = slice(y * DEPTH, (y + 1) * DEPTH)
            centre_weight = 3.0 + pot[y : y + 1, :]
            for part in range(2):
                src = pl.ds(pl.multiple_of(block * 16 + part * 8, 8), 8)
                rows = slice(part * 64, part * 64 + 64)

                def tile(ref, *index):
                    return ref[(src,) + index].astype(F32).reshape(64, DEPTH)

                centre = tile(own, y)
                down = tile(own, y - 1) if y > 0 else tile(below)
                up = tile(own, y + 1) if y < ROWS - 1 else tile(above)
                if y < ROWS // 2:
                    beside, live = tile(ahead, y), live_next
                else:
                    beside, live = tile(behind, y - ROWS // 2), live_prev
                around = lane_neighbours(centre, lane) + down + up + beside * live
                applied = centre_weight * centre - 0.5 * around
                right[block, rows, cols] = centre.astype(BF16)
                right[block, 128 + part * 64 : 192 + part * 64, cols] = applied.astype(BF16)
                near[block, rows, cols] = beside.astype(BF16)

    contract = (((1,), (1,)), ((), ()))
    half = ROWS // 2 * DEPTH

    @pl.loop(0, PAIRS)
    def _(k):
        i, j = pairs[2 * k], pairs[2 * k + 1]
        live_j = flag(support, j, plane)
        both = flag(support, i, plane) * live_j
        up_scale = -0.5 * live_j * flag(support, j, nxt) * flag(support, i, nxt)
        down_scale = -0.5 * live_j * flag(support, j, prv) * flag(support, i, prv)
        product = lax.dot_general(right[i, 0:W, :], right[j], contract, preferred_element_type=F32)
        cross_up = lax.dot_general(near[i, :, 0:half], right[j, 0:W, 0:half], contract,
                                   preferred_element_type=F32)
        cross_down = lax.dot_general(near[i, :, half:], right[j, 0:W, half:], contract,
                                     preferred_element_type=F32)
        tmp_s[...] = product[:, 0:W] * both
        tmp_h[...] = product[:, W:] * both + cross_up * up_scale + cross_down * down_scale
        group, member = k // 8, lax.rem(k, 8)
        for x in range(XD):
            keep = pl.ds(2 * x + core, ZD, stride=8)
            give = pl.ds(2 * x + 1 - core, ZD, stride=8)
            mine[x, group, member, :, 0:W] = tmp_s[keep, :]
            mine[x, group, member, :, W:] = tmp_h[keep, :]
            theirs[x, group, member, :, 0:W] = tmp_s[give, :]
            theirs[x, group, member, :, W:] = tmp_h[give, :]


def region_products(pair_flat, support_flat, where, own, ahead, behind, below, above, pot):
    vmem = pl.BlockSpec(memory_space=pltpu.VMEM)
    smem = pl.BlockSpec(memory_space=pltpu.SMEM)
    part = jax.ShapeDtypeStruct((XD, YD, 8, ZD, 2 * W), F32)
    return pl.pallas_call(
        region_kernel,
        out_shape=(part, part),
        in_specs=[smem] * 3 + [vmem] * 6,
        out_specs=(vmem, vmem),
        scratch_shapes=[
            pltpu.VMEM((NB, 2 * W, ROWS * DEPTH), BF16),
            pltpu.VMEM((NB, W, ROWS * DEPTH), BF16),
            pltpu.VMEM((W, W), F32),
            pltpu.VMEM((W, W), F32),
        ],
        compiler_params=pltpu.CompilerParams(vmem_limit_bytes=40 << 20),
        name="region_products",
    )(pair_flat, support_flat, where, own, ahead, behind, below, above, pot)


def orbital_kernel(support, where, phi, below, above, pot, out):
    block = where[2]
    lane = lax.broadcasted_iota(jnp.int32, (8, ROWS, DEPTH), 2)
    row = lax.broadcasted_iota(jnp.int32, (8, ROWS, DEPTH), 1)

    def masked(x):
        return phi[:, x].astype(F32) * flag(support, block, x)

    def step(x, carry):
        before, _ = carry
        centre = phi[:, x].astype(F32)
        after = masked(lax.rem(x + 1, PLANES))
        low = jnp.where(row == 0, below[:, x].astype(F32), pltpu.roll(centre, 1, 1))
        high = jnp.where(row == ROWS - 1, above[:, x].astype(F32), pltpu.roll(centre, ROWS - 1, 1))
        around = lane_neighbours(centre, lane) + low + high + before + after
        live = flag(support, block, x)
        applied = ((3.0 + pot[x])[None] * centre - 0.5 * around) * live
        out[:, x] = applied.astype(BF16)
        return centre * live, 0

    lax.fori_loop(0, PLANES, step, (masked(PLANES - 1), 0))


def orbital_apply(support_flat, where, phi, below, above, pot):
    vmem = pl.BlockSpec(memory_space=pltpu.VMEM)
    smem = pl.BlockSpec(memory_space=pltpu.SMEM)
    return pl.pallas_call(
        orbital_kernel,
        out_shape=jax.ShapeDtypeStruct(phi.shape, BF16),
        in_specs=[smem] * 2 + [vmem] * 4,
        out_specs=vmem,
        compiler_params=pltpu.CompilerParams(vmem_limit_bytes=24 << 20),
        name="orbital_apply",
    )(support_flat, where, phi, below, above, pot)


def ring(count, shift):
    return [(i, (i + shift) % count) for i in range(count)]


def local(phi, potential, pair_list, support):
    region = lax.axis_index(REGION)
    core = lax.axis_index("c")
    where = jnp.stack([region, core, region // 16]).astype(jnp.int32)
    pair_flat = pair_list.reshape(-1)
    support_flat = support.reshape(-1)

    own = lax.all_to_all(phi.transpose(1, 2, 0, 3), REGION, split_axis=0, concat_axis=0, tiled=True)
    ahead = lax.ppermute(own[:, :4], REGION, ring(PLANES, -1))
    behind = lax.ppermute(own[:, 4:], REGION, ring(PLANES, 1))
    below = lax.ppermute(own[:, 7], "y", ring(YD, 1))
    above = lax.ppermute(own[:, 0], "y", ring(YD, -1))
    mine, theirs = region_products(pair_flat, support_flat, where, own, ahead, behind, below, above,
                                   potential[0])
    total = mine + lax.ppermute(theirs, "c", [(0, 1), (1, 0)])
    shares = lax.all_to_all(total.reshape(XD * YD, 8, ZD, 2 * W), ("x", "y"), split_axis=0,
                            concat_axis=0, tiled=True)
    partial = jnp.sum(shares, axis=0).transpose(1, 0, 2)
    shares = lax.all_to_all(partial, ("z",), split_axis=0, concat_axis=0, tiled=True)
    result = jnp.sum(shares, axis=0)

    pot_all = lax.all_gather(potential, REGION, axis=0, tiled=True)
    row_below = lax.ppermute(phi[:, :, 7:], "y", ring(YD, 1))
    row_above = lax.ppermute(phi[:, :, :1], "y", ring(YD, -1))
    hphi = orbital_apply(support_flat, where, phi, row_below, row_above, pot_all)
    return result[:, :W], result[:, W:], hphi


def solution(mesh):
    fine = Mesh(mesh.devices.reshape(ZD, XD, CD, YD), ("z", "x", "c", "y"))
    in_specs = (P(REGION, None, "y", None), P(REGION, "y", None), P(), P())
    out_specs = (P("y", REGION), P("y", REGION), P(REGION, None, "y", None))
    return jax.shard_map(local, mesh=fine, in_specs=in_specs, out_specs=out_specs, check_vma=False)
```

```python
import functools

import jax
import jax.numpy as jnp
from jax import lax
from jax.experimental import pallas as pl
from jax.experimental.pallas import tpu as pltpu
from jax.sharding import Mesh, PartitionSpec as P

W = 128
NB = 8
ROWS = 8
DEPTH = 128
PLANES = 128
PAIRS = 32
ZD, XD, CD, YD = 16, 4, 2, 4
REGION = ("z", "x", "c")
F32 = jnp.float32
BF16 = jnp.bfloat16


def flag(support, block, plane):
    return (support[block * PLANES + plane] > 0).astype(F32)


def lane_neighbours(tile, lane):
    axis = tile.ndim - 1
    low = jnp.where(lane == 0, 0.0, pltpu.roll(tile, 1, axis))
    high = jnp.where(lane == DEPTH - 1, 0.0, pltpu.roll(tile, DEPTH - 1, axis))
    return low + high


def region_kernel(pairs, support, where, own, ahead, behind, below, above, pot,
                  mine, theirs, right, near, tmp_s, tmp_h):
    plane, core = where[0], where[1]
    nxt = lax.rem(plane + 1, PLANES)
    prv = lax.rem(plane + PLANES - 1, PLANES)
    lane = lax.broadcasted_iota(jnp.int32, (64, DEPTH), 1)

    @pl.loop(0, NB)
    def _(block):
        live_next = flag(support, block, nxt)
        live_prev = flag(support, block, prv)
        for y in range(ROWS):
            cols = slice(y * DEPTH, (y + 1) * DEPTH)
            centre_weight = 3.0 + pot[y : y + 1, :]
            for part in range(2):
                src = pl.ds(pl.multiple_of(block * 16 + part * 8, 8), 8)
                rows = slice(part * 64, part * 64 + 64)

                def tile(ref, *index):
                    return ref[(src,) + index].astype(F32).reshape(64, DEPTH)

                centre = tile(own, y)
                down = tile(own, y - 1) if y > 0 else tile(below)
                up = tile(own, y + 1) if y < ROWS - 1 else tile(above)
                if y < ROWS // 2:
                    beside, live = tile(ahead, y), live_next
                else:
                    beside, live = tile(behind, y - ROWS // 2), live_prev
                around = lane_neighbours(centre, lane) + down + up + beside * live
                applied = centre_weight * centre - 0.5 * around
                right[block, rows, cols] = centre.astype(BF16)
                right[block, 128 + part * 64 : 192 + part * 64, cols] = applied.astype(BF16)
                near[block, rows, cols] = beside.astype(BF16)

    contract = (((1,), (1,)), ((), ()))
    half = ROWS // 2 * DEPTH

    @pl.loop(0, PAIRS)
    def _(k):
        i, j = pairs[2 * k], pairs[2 * k + 1]
        live_j = flag(support, j, plane)
        both = flag(support, i, plane) * live_j
        up_scale = -0.5 * live_j * flag(support, j, nxt) * flag(support, i, nxt)
        down_scale = -0.5 * live_j * flag(support, j, prv) * flag(support, i, prv)
        product = lax.dot_general(right[i, 0:W, :], right[j], contract, preferred_element_type=F32)
        cross_up = lax.dot_general(near[i, :, 0:half], right[j, 0:W, 0:half], contract,
                                   preferred_element_type=F32)
        cross_down = lax.dot_general(near[i, :, half:], right[j, 0:W, half:], contract,
                                     preferred_element_type=F32)
        tmp_s[...] = product[:, 0:W] * both
        tmp_h[...] = product[:, W:] * both + cross_up * up_scale + cross_down * down_scale
        group, member = k // 8, lax.rem(k, 8)
        for x in range(XD):
            keep = pl.ds(2 * x + core, ZD, stride=8)
            give = pl.ds(2 * x + 1 - core, ZD, stride=8)
            mine[x, group, member, :, 0:W] = tmp_s[keep, :]
            mine[x, group, member, :, W:] = tmp_h[keep, :]
            theirs[x, group, member, :, 0:W] = tmp_s[give, :]
            theirs[x, group, member, :, W:] = tmp_h[give, :]


def region_products(pair_flat, support_flat, where, own, ahead, behind, below, above, pot):
    vmem = pl.BlockSpec(memory_space=pltpu.VMEM)
    smem = pl.BlockSpec(memory_space=pltpu.SMEM)
    part = jax.ShapeDtypeStruct((XD, YD, 8, ZD, 2 * W), F32)
    return pl.pallas_call(
        region_kernel,
        out_shape=(part, part),
        in_specs=[smem] * 3 + [vmem] * 6,
        out_specs=(vmem, vmem),
        scratch_shapes=[
            pltpu.VMEM((NB, 2 * W, ROWS * DEPTH), BF16),
            pltpu.VMEM((NB, W, ROWS * DEPTH), BF16),
            pltpu.VMEM((W, W), F32),
            pltpu.VMEM((W, W), F32),
        ],
        compiler_params=pltpu.CompilerParams(vmem_limit_bytes=40 << 20),
        name="region_products",
    )(pair_flat, support_flat, where, own, ahead, behind, below, above, pot)


def orbital_kernel(support, where, phi, below, above, pot, out):
    block = where[2]
    lane = lax.broadcasted_iota(jnp.int32, (8, ROWS, DEPTH), 2)
    row = lax.broadcasted_iota(jnp.int32, (8, ROWS, DEPTH), 1)

    def masked(x):
        return phi[:, x].astype(F32) * flag(support, block, x)

    def step(x, carry):
        before, _ = carry
        centre = phi[:, x].astype(F32)
        after = masked(lax.rem(x + 1, PLANES))
        low = jnp.where(row == 0, below[:, x].astype(F32), pltpu.roll(centre, 1, 1))
        high = jnp.where(row == ROWS - 1, above[:, x].astype(F32), pltpu.roll(centre, ROWS - 1, 1))
        around = lane_neighbours(centre, lane) + low + high + before + after
        live = flag(support, block, x)
        applied = ((3.0 + pot[lax.rem(x, 8), x // 8])[None] * centre - 0.5 * around) * live
        out[:, x] = applied.astype(BF16)
        return centre * live, 0

    lax.fori_loop(0, PLANES, step, (masked(PLANES - 1), 0))


def orbital_apply(support_flat, where, phi, below, above, pot):
    vmem = pl.BlockSpec(memory_space=pltpu.VMEM)
    smem = pl.BlockSpec(memory_space=pltpu.SMEM)
    return pl.pallas_call(
        orbital_kernel,
        out_shape=jax.ShapeDtypeStruct(phi.shape, BF16),
        in_specs=[smem] * 2 + [vmem] * 4,
        out_specs=vmem,
        compiler_params=pltpu.CompilerParams(vmem_limit_bytes=24 << 20),
        name="orbital_apply",
    )(support_flat, where, phi, below, above, pot)


def ring(count, shift):
    return [(i, (i + shift) % count) for i in range(count)]


def local(phi, potential, pair_list, support):
    region = lax.axis_index(REGION)
    core = lax.axis_index("c")
    where = jnp.stack([region, core, region // 16]).astype(jnp.int32)
    pair_flat = pair_list.reshape(-1)
    support_flat = support.reshape(-1)

    own = lax.all_to_all(phi.transpose(1, 2, 0, 3), REGION, split_axis=0, concat_axis=0, tiled=True)
    column = lax.all_gather(potential, "z", axis=0, tiled=True)
    pot_all = lax.all_gather(column[None], ("x", "c"), axis=0, tiled=True)
    row_below = lax.ppermute(phi[:, :, 7:], "y", ring(YD, 1))
    row_above = lax.ppermute(phi[:, :, :1], "y", ring(YD, -1))
    hphi = orbital_apply(support_flat, where, phi, row_below, row_above, pot_all)
    own, hphi = lax.optimization_barrier((own, hphi))
    ahead = lax.ppermute(own[:, :4], REGION, ring(PLANES, -1))
    behind = lax.ppermute(own[:, 4:], REGION, ring(PLANES, 1))
    below = lax.ppermute(own[:, 7], "y", ring(YD, 1))
    above = lax.ppermute(own[:, 0], "y", ring(YD, -1))
    mine, theirs = region_products(pair_flat, support_flat, where, own, ahead, behind, below, above,
                                   potential[0])
    total = mine + lax.ppermute(theirs, "c", [(0, 1), (1, 0)])
    shares = lax.all_to_all(total.reshape(XD * YD, 8, ZD, 2 * W), ("x", "y"), split_axis=0,
                            concat_axis=0, tiled=True)
    partial = jnp.sum(shares, axis=0).transpose(1, 0, 2)
    shares = lax.all_to_all(partial, ("z",), split_axis=0, concat_axis=0, tiled=True)
    result = jnp.sum(shares, axis=0)

    return result[:, :W], result[:, W:], hphi


def solution(mesh):
    fine = Mesh(mesh.devices.reshape(ZD, XD, CD, YD), ("z", "x", "c", "y"))
    in_specs = (P(REGION, None, "y", None), P(REGION, "y", None), P(), P())
    out_specs = (P("y", REGION), P("y", REGION), P(REGION, None, "y", None))
    return jax.shard_map(local, mesh=fine, in_specs=in_specs, out_specs=out_specs, check_vma=False)
```

```python
import functools

import jax
import jax.numpy as jnp
from jax import lax
from jax.experimental import pallas as pl
from jax.experimental.pallas import tpu as pltpu
from jax.sharding import Mesh, PartitionSpec as P

W = 128
NB = 8
ROWS = 8
DEPTH = 128
PLANES = 128
PAIRS = 32
ZD, XD, CD, YD = 16, 4, 2, 4
REGION = ("z", "x", "c")
F32 = jnp.float32
BF16 = jnp.bfloat16


def flag(support, block, plane):
    return (support[block * PLANES + plane] > 0).astype(F32)


def lane_neighbours(tile, lane):
    axis = tile.ndim - 1
    low = jnp.where(lane == 0, 0.0, pltpu.roll(tile, 1, axis))
    high = jnp.where(lane == DEPTH - 1, 0.0, pltpu.roll(tile, DEPTH - 1, axis))
    return low + high


def split_rows(pairs, gram, core, mine, theirs):
    @pl.loop(0, PAIRS)
    def _(k):
        i, j = pairs[2 * k], pairs[2 * k + 1]
        group, member = k // 8, lax.rem(k, 8)
        for x in range(XD):
            mine[x, group, member] = gram[j, pl.ds(i * W + 2 * x + core, ZD, stride=8), :]
            theirs[x, group, member] = gram[j, pl.ds(i * W + 2 * x + 1 - core, ZD, stride=8), :]


def gram_blocks(left, right, gram):
    @pl.loop(0, NB // 2)
    def _(n):
        cols = pl.ds(pl.multiple_of(n * 2 * W, 2 * W), 2 * W)
        product = lax.dot_general(left[...], right[cols, :], (((1,), (1,)), ((), ())),
                                  preferred_element_type=F32)
        gram[2 * n] = product[:, 0:W]
        gram[2 * n + 1] = product[:, W:]


def overlap_kernel(pairs, support, where, own, conf, mine, theirs, gram):
    plane, core = where[0], where[1]

    @pl.loop(0, NB)
    def _(block):
        live = flag(support, block, plane)
        for y in range(ROWS):
            tile = own[pl.ds(block * 16, 16), y].astype(F32).reshape(W, DEPTH) * live
            conf[pl.ds(pl.multiple_of(block * W, W), W), y * DEPTH : (y + 1) * DEPTH] = tile.astype(BF16)

    gram_blocks(conf, conf, gram)
    split_rows(pairs, gram, core, mine, theirs)


def hamiltonian_kernel(pairs, support, where, conf, ahead, behind, above, pot,
                       mine, theirs, left, right, gram):
    plane, core = where[0], where[1]
    nxt = lax.rem(plane + 1, PLANES)
    prv = lax.rem(plane + PLANES - 1, PLANES)
    lane = lax.broadcasted_iota(jnp.int32, (64, DEPTH), 1)
    full = ROWS * DEPTH

    @pl.loop(0, 2 * NB)
    def _(half):
        block = half // 2
        live = flag(support, block, plane)
        live_next = flag(support, block, nxt)
        live_prev = flag(support, block, prv)
        src = pl.ds(pl.multiple_of(half * 8, 8), 8)
        rows = pl.ds(pl.multiple_of(half * 64, 64), 64)

        def row_of(y):
            return conf[rows, y * DEPTH : (y + 1) * DEPTH].astype(F32)

        def tile(ref, *index):
            return ref[(src,) + index].astype(F32).reshape(64, DEPTH)

        edge = tile(above) * live
        for y in range(ROWS):
            cols = slice(y * DEPTH, (y + 1) * DEPTH)
            more = slice(full + y * DEPTH, full + (y + 1) * DEPTH)
            centre = row_of(y)
            if y < ROWS // 2:
                beside, live_there = tile(ahead, y) * live_next, live_next
            else:
                beside, live_there = tile(behind, y - ROWS // 2) * live_prev, live_prev
            around = lane_neighbours(centre, lane) + beside * live
            around = around + (row_of(y + 1) if y < ROWS - 1 else edge)
            if y > 0:
                around = around + row_of(y - 1)
            applied = (3.0 + pot[y : y + 1, :]) * centre - 0.5 * around
            left[rows, cols] = centre.astype(BF16)
            left[rows, more] = beside.astype(BF16)
            right[rows, cols] = applied.astype(BF16)
            right[rows, more] = (centre * (-0.5 * live_there)).astype(BF16)
        last = slice(2 * full, 2 * full + DEPTH)
        left[rows, last] = edge.astype(BF16)
        right[rows, last] = (row_of(ROWS - 1) * -0.5).astype(BF16)

    gram_blocks(left, right, gram)
    split_rows(pairs, gram, core, mine, theirs)


VMEM = pl.BlockSpec(memory_space=pltpu.VMEM)
SMEM = pl.BlockSpec(memory_space=pltpu.SMEM)
SHARE = jax.ShapeDtypeStruct((XD, YD, 8, ZD, W), F32)
CELLS = ROWS * DEPTH


def overlap_products(pair_flat, support_flat, where, own):
    return pl.pallas_call(
        overlap_kernel,
        out_shape=(jax.ShapeDtypeStruct((NB * W, CELLS), BF16), SHARE, SHARE),
        in_specs=[SMEM] * 3 + [VMEM],
        out_specs=(VMEM,) * 3,
        scratch_shapes=[pltpu.VMEM((NB, NB * W, W), F32)],
        compiler_params=pltpu.CompilerParams(vmem_limit_bytes=20 << 20),
        name="overlap_products",
    )(pair_flat, support_flat, where, own)


def hamiltonian_products(pair_flat, support_flat, where, conf, ahead, behind, above, pot):
    return pl.pallas_call(
        hamiltonian_kernel,
        out_shape=(SHARE, SHARE),
        in_specs=[SMEM] * 3 + [VMEM] * 5,
        out_specs=(VMEM,) * 2,
        scratch_shapes=[
            pltpu.VMEM((NB * W, 2 * CELLS + DEPTH), BF16),
            pltpu.VMEM((NB * W, 2 * CELLS + DEPTH), BF16),
            pltpu.VMEM((NB, NB * W, W), F32),
        ],
        compiler_params=pltpu.CompilerParams(vmem_limit_bytes=32 << 20),
        name="hamiltonian_products",
    )(pair_flat, support_flat, where, conf, ahead, behind, above, pot)


def orbital_kernel(support, where, phi, below, above, pot, out):
    block, row_z = where[2], where[0] // 8
    lane = lax.broadcasted_iota(jnp.int32, (8, ROWS, DEPTH), 2)
    row = lax.broadcasted_iota(jnp.int32, (8, ROWS, DEPTH), 1)

    def masked(x):
        return phi[:, x].astype(F32) * flag(support, block, x)

    def step(x, carry):
        before, _ = carry
        centre = phi[:, x].astype(F32)
        after = masked(lax.rem(x + 1, PLANES))
        low = jnp.where(row == 0, below[:, x].astype(F32), pltpu.roll(centre, 1, 1))
        high = jnp.where(row == ROWS - 1, above[:, x].astype(F32), pltpu.roll(centre, ROWS - 1, 1))
        around = lane_neighbours(centre, lane) + low + high + before + after
        live = flag(support, block, x)
        applied = ((3.0 + pot[lax.rem(x, 8), lax.rem(x // 8 + ZD - row_z, ZD)])[None] * centre - 0.5 * around) * live
        out[:, x] = applied.astype(BF16)
        return centre * live, 0

    lax.fori_loop(0, PLANES, step, (masked(PLANES - 1), 0))


def orbital_apply(support_flat, where, phi, below, above, pot):
    return pl.pallas_call(
        orbital_kernel,
        out_shape=jax.ShapeDtypeStruct(phi.shape, BF16),
        in_specs=[SMEM] * 2 + [VMEM] * 4,
        out_specs=VMEM,
        compiler_params=pltpu.CompilerParams(vmem_limit_bytes=24 << 20),
        name="orbital_apply",
    )(support_flat, where, phi, below, above, pot)


def ring(count, shift):
    return [(i, (i + shift) % count) for i in range(count)]


def local(phi, potential, pair_list, support):
    region = lax.axis_index(REGION)
    core = lax.axis_index("c")
    where = jnp.stack([region, core, region // 16]).astype(jnp.int32)
    pair_flat = pair_list.reshape(-1)
    support_flat = support.reshape(-1)

    own = lax.all_to_all(phi.transpose(1, 2, 0, 3), REGION, split_axis=0, concat_axis=0, tiled=True)

    column = potential
    for step in (1, 2, 4, 8):
        column = jnp.concatenate([column, lax.ppermute(column, "z", ring(ZD, -step))], axis=0)
    pot_all = lax.all_gather(column[None], ("x", "c"), axis=0, tiled=True)
    row_below = lax.ppermute(phi[:, :, 7:], "y", ring(YD, 1))
    row_above = lax.ppermute(phi[:, :, :1], "y", ring(YD, -1))
    hphi = orbital_apply(support_flat, where, phi, row_below, row_above, pot_all)
    own, hphi = lax.optimization_barrier((own, hphi))

    ahead = lax.ppermute(own[:, :4], REGION, ring(PLANES, -1))
    behind = lax.ppermute(own[:, 4:], REGION, ring(PLANES, 1))
    above = lax.ppermute(own[:, 0], "y", ring(YD, -1))
    conf, mine_s, theirs_s = overlap_products(pair_flat, support_flat, where, own)
    swap = [(0, 1), (1, 0)]
    total_s = mine_s + lax.ppermute(theirs_s, "c", swap)
    mine_h, theirs_h = hamiltonian_products(pair_flat, support_flat, where, conf, ahead, behind, above,
                                            potential[0])
    total_h = mine_h + lax.ppermute(theirs_h, "c", swap)
    total = jnp.stack([total_s, total_h], axis=2).reshape(XD * YD, 2, 8, ZD, W)
    shares = lax.all_to_all(total, ("x", "y"), split_axis=0, concat_axis=0, tiled=True)
    partial = jnp.sum(shares, axis=0).transpose(2, 0, 1, 3)
    shares = lax.all_to_all(partial, ("z",), split_axis=0, concat_axis=0, tiled=True)
    result = jnp.sum(shares, axis=0)
    return result[0], result[1], hphi


def solution(mesh):
    fine = Mesh(mesh.devices.reshape(ZD, XD, CD, YD), ("z", "x", "c", "y"))
    in_specs = (P(REGION, None, "y", None), P(REGION, "y", None), P(), P())
    out_specs = (P("y", REGION), P("y", REGION), P(REGION, None, "y", None))
    return jax.shard_map(local, mesh=fine, in_specs=in_specs, out_specs=out_specs, check_vma=False)
```

```python
import functools

import jax
import jax.numpy as jnp
from jax import lax
from jax.experimental import pallas as pl
from jax.experimental.pallas import tpu as pltpu
from jax.sharding import Mesh, PartitionSpec as P

W = 128
NB = 8
ROWS = 8
DEPTH = 128
PLANES = 128
PAIRS = 32
ZD, XD, CD, YD = 16, 4, 2, 4
REGION = ("z", "x", "c")
F32 = jnp.float32
BF16 = jnp.bfloat16


def flag(support, block, plane):
    return (support[block * PLANES + plane] > 0).astype(F32)


def lane_neighbours(tile, lane):
    axis = tile.ndim - 1
    low = jnp.where(lane == 0, 0.0, pltpu.roll(tile, 1, axis))
    high = jnp.where(lane == DEPTH - 1, 0.0, pltpu.roll(tile, DEPTH - 1, axis))
    return low + high


def split_rows(pairs, gram, core, mine, theirs):
    @pl.loop(0, PAIRS)
    def _(k):
        i, j = pairs[2 * k], pairs[2 * k + 1]
        group, member = k // 8, lax.rem(k, 8)
        for x in range(XD):
            mine[x, group, member] = gram[j, pl.ds(i * W + 2 * x + core, ZD, stride=8), :]
            theirs[x, group, member] = gram[j, pl.ds(i * W + 2 * x + 1 - core, ZD, stride=8), :]


def gram_blocks(left, right, gram):
    @pl.loop(0, NB // 2)
    def _(n):
        cols = pl.ds(pl.multiple_of(n * 2 * W, 2 * W), 2 * W)
        product = lax.dot_general(left[...], right[cols, :], (((1,), (1,)), ((), ())),
                                  preferred_element_type=F32)
        gram[2 * n] = product[:, 0:W]
        gram[2 * n + 1] = product[:, W:]


def overlap_kernel(pairs, support, where, own, conf, mine, theirs, gram):
    plane, core = where[0], where[1]

    @pl.loop(0, NB)
    def _(block):
        live = flag(support, block, plane)
        for y in range(ROWS):
            tile = own[pl.ds(block * 16, 16), y].astype(F32).reshape(W, DEPTH) * live
            conf[pl.ds(pl.multiple_of(block * W, W), W), y * DEPTH : (y + 1) * DEPTH] = tile.astype(BF16)

    gram_blocks(conf, conf, gram)
    split_rows(pairs, gram, core, mine, theirs)


def hamiltonian_kernel(pairs, support, where, conf, ahead, behind, above, pot,
                       mine, theirs, left, right, gram):
    plane, core = where[0], where[1]
    nxt = lax.rem(plane + 1, PLANES)
    prv = lax.rem(plane + PLANES - 1, PLANES)
    lane = lax.broadcasted_iota(jnp.int32, (64, DEPTH), 1)
    full = ROWS * DEPTH

    @pl.loop(0, 2 * NB)
    def _(half):
        block = half // 2
        live = flag(support, block, plane)
        live_next = flag(support, block, nxt)
        live_prev = flag(support, block, prv)
        src = pl.ds(pl.multiple_of(half * 8, 8), 8)
        rows = pl.ds(pl.multiple_of(half * 64, 64), 64)

        def row_of(y):
            return conf[rows, y * DEPTH : (y + 1) * DEPTH].astype(F32)

        def tile(ref, *index):
            return ref[(src,) + index].astype(F32).reshape(64, DEPTH)

        edge = tile(above) * live
        for y in range(ROWS):
            cols = slice(y * DEPTH, (y + 1) * DEPTH)
            more = slice(full + y * DEPTH, full + (y + 1) * DEPTH)
            centre = row_of(y)
            if y < ROWS // 2:
                beside, live_there = tile(ahead, y) * live_next, live_next
            else:
                beside, live_there = tile(behind, y - ROWS // 2) * live_prev, live_prev
            around = lane_neighbours(centre, lane) + beside * live
            around = around + (row_of(y + 1) if y < ROWS - 1 else edge)
            if y > 0:
                around = around + row_of(y - 1)
            applied = (3.0 + pot[y : y + 1, :]) * centre - 0.5 * around
            left[rows, cols] = centre.astype(BF16)
            left[rows, more] = beside.astype(BF16)
            right[rows, cols] = applied.astype(BF16)
            right[rows, more] = (centre * (-0.5 * live_there)).astype(BF16)
        last = slice(2 * full, 2 * full + DEPTH)
        left[rows, last] = edge.astype(BF16)
        right[rows, last] = (row_of(ROWS - 1) * -0.5).astype(BF16)

    gram_blocks(left, right, gram)
    split_rows(pairs, gram, core, mine, theirs)


VMEM = pl.BlockSpec(memory_space=pltpu.VMEM)
SMEM = pl.BlockSpec(memory_space=pltpu.SMEM)
SHARE = jax.ShapeDtypeStruct((XD, YD, 8, ZD, W), F32)
CELLS = ROWS * DEPTH


def overlap_products(pair_flat, support_flat, where, own):
    return pl.pallas_call(
        overlap_kernel,
        out_shape=(jax.ShapeDtypeStruct((NB * W, CELLS), BF16), SHARE, SHARE),
        in_specs=[SMEM] * 3 + [VMEM],
        out_specs=(VMEM,) * 3,
        scratch_shapes=[pltpu.VMEM((NB, NB * W, W), F32)],
        compiler_params=pltpu.CompilerParams(vmem_limit_bytes=16 << 20),
        name="overlap_products",
    )(pair_flat, support_flat, where, own)


def hamiltonian_products(pair_flat, support_flat, where, conf, ahead, behind, above, pot):
    return pl.pallas_call(
        hamiltonian_kernel,
        out_shape=(SHARE, SHARE),
        in_specs=[SMEM] * 3 + [VMEM] * 5,
        out_specs=(VMEM,) * 2,
        scratch_shapes=[
            pltpu.VMEM((NB * W, 2 * CELLS + DEPTH), BF16),
            pltpu.VMEM((NB * W, 2 * CELLS + DEPTH), BF16),
            pltpu.VMEM((NB, NB * W, W), F32),
        ],
        compiler_params=pltpu.CompilerParams(vmem_limit_bytes=26 << 20),
        name="hamiltonian_products",
    )(pair_flat, support_flat, where, conf, ahead, behind, above, pot)


def kinetic_kernel(support, where, phi, below, above, out):
    block = where[2]
    lane = lax.broadcasted_iota(jnp.int32, (8, ROWS, DEPTH), 2)
    row = lax.broadcasted_iota(jnp.int32, (8, ROWS, DEPTH), 1)

    def masked(x):
        return phi[:, x].astype(F32) * flag(support, block, x)

    def step(x, carry):
        before, centre = carry
        after = masked(lax.rem(x + 1, PLANES))
        low = jnp.where(row == 0, below[:, x].astype(F32), pltpu.roll(centre, 1, 1))
        high = jnp.where(row == ROWS - 1, above[:, x].astype(F32), pltpu.roll(centre, ROWS - 1, 1))
        around = lane_neighbours(centre, lane) + low + high + before + after
        live = flag(support, block, x)
        out[x] = (3.0 * centre - 0.5 * around) * live
        return centre, after

    lax.fori_loop(0, PLANES, step, (masked(PLANES - 1), masked(0)))


def potential_kernel(support, where, kinetic, phi, pot, out):
    block = where[2]

    @pl.loop(0, PLANES)
    def _(x):
        values = pot[x // 8, 0, lax.rem(x, 8)] * flag(support, block, x)
        out[:, x] = (kinetic[x] + values[None] * phi[:, x].astype(F32)).astype(BF16)


def kinetic_part(support_flat, where, phi, below, above):
    return pl.pallas_call(
        kinetic_kernel,
        out_shape=jax.ShapeDtypeStruct((PLANES, 8, ROWS, DEPTH), F32),
        in_specs=[SMEM] * 2 + [VMEM] * 3,
        out_specs=VMEM,
        compiler_params=pltpu.CompilerParams(vmem_limit_bytes=10 << 20),
        name="kinetic_part",
    )(support_flat, where, phi, below, above)


def potential_part(support_flat, where, kinetic, phi, pot):
    return pl.pallas_call(
        potential_kernel,
        out_shape=jax.ShapeDtypeStruct(phi.shape, BF16),
        in_specs=[SMEM] * 2 + [VMEM] * 3,
        out_specs=VMEM,
        compiler_params=pltpu.CompilerParams(vmem_limit_bytes=14 << 20),
        name="potential_part",
    )(support_flat, where, kinetic, phi, pot)


def ring(count, shift):
    return [(i, (i + shift) % count) for i in range(count)]


def local(phi, potential, pair_list, support):
    region = lax.axis_index(REGION)
    core = lax.axis_index("c")
    where = jnp.stack([region, core, region // 16]).astype(jnp.int32)
    pair_flat = pair_list.reshape(-1)
    support_flat = support.reshape(-1)

    own = lax.all_to_all(phi.transpose(1, 2, 0, 3), REGION, split_axis=0, concat_axis=0, tiled=True)

    plane_row = lax.all_gather(potential, ("x", "c"), axis=0, tiled=True)
    row_below = lax.ppermute(phi[:, :, 7:], "y", ring(YD, 1))
    row_above = lax.ppermute(phi[:, :, :1], "y", ring(YD, -1))
    kinetic = kinetic_part(support_flat, where, phi, row_below, row_above)
    own, plane_row, kinetic = lax.optimization_barrier((own, plane_row, kinetic))
    pot_all = lax.all_gather(jnp.stack([plane_row, plane_row])[None], "z", axis=0, tiled=True)

    ahead = lax.ppermute(own[:, :4], REGION, ring(PLANES, -1))
    behind = lax.ppermute(own[:, 4:], REGION, ring(PLANES, 1))
    above = lax.ppermute(own[:, 0], "y", ring(YD, -1))
    conf, mine_s, theirs_s = overlap_products(pair_flat, support_flat, where, own)
    swap = [(0, 1), (1, 0)]
    total_s = mine_s + lax.ppermute(theirs_s, "c", swap)
    mine_h, theirs_h = hamiltonian_products(pair_flat, support_flat, where, conf, ahead, behind, above,
                                            potential[0])
    total_h = mine_h + lax.ppermute(theirs_h, "c", swap)
    total = jnp.stack([total_s, total_h], axis=2).reshape(XD * YD, 2, 8, ZD, W).astype(BF16)
    shares = lax.all_to_all(total, ("x", "y"), split_axis=0, concat_axis=0, tiled=True)
    partial = jnp.sum(shares.astype(F32), axis=0).transpose(2, 0, 1, 3)
    hphi = potential_part(support_flat, where, kinetic, phi, pot_all)
    shares = lax.all_to_all(partial, ("z",), split_axis=0, concat_axis=0, tiled=True)
    result = jnp.sum(shares, axis=0)
    return result[0], result[1], hphi


def solution(mesh):
    fine = Mesh(mesh.devices.reshape(ZD, XD, CD, YD), ("z", "x", "c", "y"))
    in_specs = (P(REGION, None, "y", None), P(REGION, "y", None), P(), P())
    out_specs = (P("y", REGION), P("y", REGION), P(REGION, None, "y", None))
    return jax.shard_map(local, mesh=fine, in_specs=in_specs, out_specs=out_specs, check_vma=False)
```

```python
import functools

import jax
import jax.numpy as jnp
from jax import lax
from jax.experimental import pallas as pl
from jax.experimental.pallas import tpu as pltpu
from jax.sharding import Mesh, PartitionSpec as P

W = 128
NB = 8
ROWS = 8
DEPTH = 128
PLANES = 128
PAIRS = 32
ZD, XD, CD, YD = 16, 4, 2, 4
REGION = ("z", "x", "c")
NEAR = 6
F32 = jnp.float32
BF16 = jnp.bfloat16


def flag(support, block, plane):
    return (support[block * PLANES + plane] > 0).astype(F32)


def lane_neighbours(tile, lane):
    axis = tile.ndim - 1
    low = jnp.where(lane == 0, 0.0, pltpu.roll(tile, 1, axis))
    high = jnp.where(lane == DEPTH - 1, 0.0, pltpu.roll(tile, DEPTH - 1, axis))
    return low + high


def split_rows(pairs, gram, core, mine, theirs):
    @pl.loop(0, PAIRS)
    def _(k):
        i, j = pairs[2 * k], pairs[2 * k + 1]
        group, member = k // 8, lax.rem(k, 8)
        for x in range(XD):
            mine[x, group, member] = gram[j, pl.ds(i * W + 2 * x + core, ZD, stride=8), :]
            theirs[x, group, member] = gram[j, pl.ds(i * W + 2 * x + 1 - core, ZD, stride=8), :]


def gram_blocks(left, right, gram):
    @pl.loop(0, NB // 2)
    def _(n):
        cols = pl.ds(pl.multiple_of(n * 2 * W, 2 * W), 2 * W)
        product = lax.dot_general(left[...], right[cols, :], (((1,), (1,)), ((), ())),
                                  preferred_element_type=F32)
        gram[2 * n] = product[:, 0:W]
        gram[2 * n + 1] = product[:, W:]


def overlap_kernel(pairs, support, where, own, conf, mine, theirs, gram):
    plane, core = where[0], where[1]

    @pl.loop(0, NB)
    def _(block):
        live = flag(support, block, plane)
        for y in range(ROWS):
            tile = own[pl.ds(block * 16, 16), y].astype(F32).reshape(W, DEPTH) * live
            conf[pl.ds(pl.multiple_of(block * W, W), W), y * DEPTH : (y + 1) * DEPTH] = tile.astype(BF16)

    gram_blocks(conf, conf, gram)
    split_rows(pairs, gram, core, mine, theirs)


def hamiltonian_kernel(pairs, support, where, conf, ahead, behind, above, pot,
                       mine, theirs, left, right, gram):
    plane, core = where[0], where[1]
    nxt = lax.rem(plane + 1, PLANES)
    prv = lax.rem(plane + PLANES - 1, PLANES)
    lane = lax.broadcasted_iota(jnp.int32, (64, DEPTH), 1)
    full = ROWS * DEPTH

    @pl.loop(0, 2 * NB)
    def _(half):
        block = half // 2
        live = flag(support, block, plane)
        live_next = flag(support, block, nxt)
        live_prev = flag(support, block, prv)
        src = pl.ds(pl.multiple_of(half * 8, 8), 8)
        rows = pl.ds(pl.multiple_of(half * 64, 64), 64)

        def row_of(y):
            return conf[rows, y * DEPTH : (y + 1) * DEPTH].astype(F32)

        def tile(ref, *index):
            return ref[(src,) + index].astype(F32).reshape(64, DEPTH)

        edge = tile(above) * live
        for y in range(ROWS):
            cols = slice(y * DEPTH, (y + 1) * DEPTH)
            more = slice(full + y * DEPTH, full + (y + 1) * DEPTH)
            centre = row_of(y)
            if y < ROWS // 2:
                beside, live_there = tile(ahead, y) * live_next, live_next
            else:
                beside, live_there = tile(behind, y - ROWS // 2) * live_prev, live_prev
            around = lane_neighbours(centre, lane) + beside * live
            around = around + (row_of(y + 1) if y < ROWS - 1 else edge)
            if y > 0:
                around = around + row_of(y - 1)
            applied = (3.0 + pot[y : y + 1, :]) * centre - 0.5 * around
            left[rows, cols] = centre.astype(BF16)
            left[rows, more] = beside.astype(BF16)
            right[rows, cols] = applied.astype(BF16)
            right[rows, more] = (centre * (-0.5 * live_there)).astype(BF16)
        last = slice(2 * full, 2 * full + DEPTH)
        left[rows, last] = edge.astype(BF16)
        right[rows, last] = (row_of(ROWS - 1) * -0.5).astype(BF16)

    gram_blocks(left, right, gram)
    split_rows(pairs, gram, core, mine, theirs)


VMEM = pl.BlockSpec(memory_space=pltpu.VMEM)
SMEM = pl.BlockSpec(memory_space=pltpu.SMEM)
SHARE = jax.ShapeDtypeStruct((XD, YD, 8, ZD, W), F32)
CELLS = ROWS * DEPTH


def overlap_products(pair_flat, support_flat, where, own):
    return pl.pallas_call(
        overlap_kernel,
        out_shape=(jax.ShapeDtypeStruct((NB * W, CELLS), BF16), SHARE, SHARE),
        in_specs=[SMEM] * 3 + [VMEM],
        out_specs=(VMEM,) * 3,
        scratch_shapes=[pltpu.VMEM((NB, NB * W, W), F32)],
        compiler_params=pltpu.CompilerParams(vmem_limit_bytes=16 << 20),
        name="overlap_products",
    )(pair_flat, support_flat, where, own)


def hamiltonian_products(pair_flat, support_flat, where, conf, ahead, behind, above, pot):
    return pl.pallas_call(
        hamiltonian_kernel,
        out_shape=(SHARE, SHARE),
        in_specs=[SMEM] * 3 + [VMEM] * 5,
        out_specs=(VMEM,) * 2,
        scratch_shapes=[
            pltpu.VMEM((NB * W, 2 * CELLS + DEPTH), BF16),
            pltpu.VMEM((NB * W, 2 * CELLS + DEPTH), BF16),
            pltpu.VMEM((NB, NB * W, W), F32),
        ],
        compiler_params=pltpu.CompilerParams(vmem_limit_bytes=26 << 20),
        name="hamiltonian_products",
    )(pair_flat, support_flat, where, conf, ahead, behind, above, pot)


def orbital_kernel(support, where, phi, below, above, pot_low, pot_mid, pot_high, out, pot):
    block, row_z = where[2], where[0] // 8
    for step, piece in enumerate((pot_low, pot_mid, pot_high)):
        pot[step * NEAR : (step + 1) * NEAR] = piece[...]
    lane = lax.broadcasted_iota(jnp.int32, (8, ROWS, DEPTH), 2)
    row = lax.broadcasted_iota(jnp.int32, (8, ROWS, DEPTH), 1)

    def masked(x):
        return phi[:, x].astype(F32) * flag(support, block, x)

    def step(x, carry):
        before, _ = carry
        centre = phi[:, x].astype(F32)
        after = masked(lax.rem(x + 1, PLANES))
        low = jnp.where(row == 0, below[:, x].astype(F32), pltpu.roll(centre, 1, 1))
        high = jnp.where(row == ROWS - 1, above[:, x].astype(F32), pltpu.roll(centre, ROWS - 1, 1))
        around = lane_neighbours(centre, lane) + low + high + before + after
        live = flag(support, block, x)
        values = pot[lax.rem(x // 8 - row_z + 3 * ZD // 2, ZD), lax.rem(x, 8)]
        applied = ((3.0 + values)[None] * centre - 0.5 * around) * live
        out[:, x] = applied.astype(BF16)
        return centre * live, 0

    lax.fori_loop(0, PLANES, step, (masked(PLANES - 1), 0))


def orbital_apply(support_flat, where, phi, below, above, pieces):
    return pl.pallas_call(
        orbital_kernel,
        out_shape=jax.ShapeDtypeStruct(phi.shape, BF16),
        in_specs=[SMEM] * 2 + [VMEM] * 6,
        out_specs=VMEM,
        scratch_shapes=[pltpu.VMEM((3 * NEAR, 8, ROWS, DEPTH), F32)],
        compiler_params=pltpu.CompilerParams(vmem_limit_bytes=14 << 20),
        name="orbital_apply",
    )(support_flat, where, phi, below, above, *pieces)


def ring(count, shift):
    return [(i, (i + shift) % count) for i in range(count)]


def local(phi, potential, pair_list, support):
    region = lax.axis_index(REGION)
    core = lax.axis_index("c")
    where = jnp.stack([region, core, region // 16]).astype(jnp.int32)
    pair_flat = pair_list.reshape(-1)
    support_flat = support.reshape(-1)

    own = lax.all_to_all(phi.transpose(1, 2, 0, 3), REGION, split_axis=0, concat_axis=0, tiled=True)

    plane_row = lax.all_gather(potential, ("x", "c"), axis=0, tiled=True)
    row_below = lax.ppermute(phi[:, :, 7:], "y", ring(YD, 1))
    row_above = lax.ppermute(phi[:, :, :1], "y", ring(YD, -1))
    plane_row, row_below, row_above = lax.optimization_barrier((plane_row, row_below, row_above))
    near = [plane_row if s == 0 else lax.ppermute(plane_row, "z", ring(ZD, -s))
            for s in range(-2, NEAR - 2)]
    own, near = lax.optimization_barrier((own, near))

    ahead = lax.ppermute(own[:, :4], REGION, ring(PLANES, -1))
    behind = lax.ppermute(own[:, 4:], REGION, ring(PLANES, 1))
    above = lax.ppermute(own[:, 0], "y", ring(YD, -1))
    conf, mine_s, theirs_s = overlap_products(pair_flat, support_flat, where, own)
    swap = [(0, 1), (1, 0)]
    total_s = mine_s + lax.ppermute(theirs_s, "c", swap)
    mine_h, theirs_h = hamiltonian_products(pair_flat, support_flat, where, conf, ahead, behind, above,
                                            potential[0])
    total_h = mine_h + lax.ppermute(theirs_h, "c", swap)
    total = jnp.stack([total_s, total_h], axis=2).reshape(XD * YD, 2, 8, ZD, W).astype(BF16)
    total, near = lax.optimization_barrier((total, near))
    column = jnp.stack(near)
    pieces = [lax.ppermute(column, "z", ring(ZD, NEAR)), column,
              lax.ppermute(column, "z", ring(ZD, -NEAR))]
    shares = lax.all_to_all(total, ("x", "y"), split_axis=0, concat_axis=0, tiled=True)
    partial = jnp.sum(shares.astype(F32), axis=0).transpose(2, 0, 1, 3)
    partial, pieces = lax.optimization_barrier((partial, pieces))
    hphi = orbital_apply(support_flat, where, phi, row_below, row_above, pieces)
    shares = lax.all_to_all(partial, ("z",), split_axis=0, concat_axis=0, tiled=True)
    result = jnp.sum(shares, axis=0)
    return result[0], result[1], hphi


def solution(mesh):
    fine = Mesh(mesh.devices.reshape(ZD, XD, CD, YD), ("z", "x", "c", "y"))
    in_specs = (P(REGION, None, "y", None), P(REGION, "y", None), P(), P())
    out_specs = (P("y", REGION), P("y", REGION), P(REGION, None, "y", None))
    return jax.shard_map(local, mesh=fine, in_specs=in_specs, out_specs=out_specs, check_vma=False)
```

```python
import functools

import jax
import jax.numpy as jnp
from jax import lax
from jax.experimental import pallas as pl
from jax.experimental.pallas import tpu as pltpu
from jax.sharding import Mesh, PartitionSpec as P

W = 128
NB = 8
ROWS = 8
DEPTH = 128
PLANES = 128
PAIRS = 32
ZD, XD, CD, YD = 16, 4, 2, 4
REGION = ("z", "x", "c")
STRIDE = (0, 3, 6, 9, 12, 15)
F32 = jnp.float32
BF16 = jnp.bfloat16


def flag(support, block, plane):
    return (support[block * PLANES + plane] > 0).astype(F32)


def lane_neighbours(tile, lane):
    axis = tile.ndim - 1
    low = jnp.where(lane == 0, 0.0, pltpu.roll(tile, 1, axis))
    high = jnp.where(lane == DEPTH - 1, 0.0, pltpu.roll(tile, DEPTH - 1, axis))
    return low + high


def split_rows(pairs, gram, core, mine, theirs):
    @pl.loop(0, PAIRS)
    def _(k):
        i, j = pairs[2 * k], pairs[2 * k + 1]
        group, member = k // 8, lax.rem(k, 8)
        for x in range(XD):
            mine[x, group, member] = gram[j, pl.ds(i * W + 2 * x + core, ZD, stride=8), :]
            theirs[x, group, member] = gram[j, pl.ds(i * W + 2 * x + 1 - core, ZD, stride=8), :]


def gram_blocks(left, right, gram):
    @pl.loop(0, NB // 2)
    def _(n):
        cols = pl.ds(pl.multiple_of(n * 2 * W, 2 * W), 2 * W)
        product = lax.dot_general(left[...], right[cols, :], (((1,), (1,)), ((), ())),
                                  preferred_element_type=F32)
        gram[2 * n] = product[:, 0:W]
        gram[2 * n + 1] = product[:, W:]


def overlap_kernel(pairs, support, where, own, conf, mine, theirs, gram):
    plane, core = where[0], where[1]

    @pl.loop(0, NB)
    def _(block):
        live = flag(support, block, plane)
        for y in range(ROWS):
            tile = own[pl.ds(block * 16, 16), y].astype(F32).reshape(W, DEPTH) * live
            conf[pl.ds(pl.multiple_of(block * W, W), W), y * DEPTH : (y + 1) * DEPTH] = tile.astype(BF16)

    gram_blocks(conf, conf, gram)
    split_rows(pairs, gram, core, mine, theirs)


def hamiltonian_kernel(pairs, support, where, conf, ahead, behind, above, pot,
                       mine, theirs, left, right, gram):
    plane, core = where[0], where[1]
    nxt = lax.rem(plane + 1, PLANES)
    prv = lax.rem(plane + PLANES - 1, PLANES)
    lane = lax.broadcasted_iota(jnp.int32, (64, DEPTH), 1)
    full = ROWS * DEPTH

    @pl.loop(0, 2 * NB)
    def _(half):
        block = half // 2
        live = flag(support, block, plane)
        live_next = flag(support, block, nxt)
        live_prev = flag(support, block, prv)
        src = pl.ds(pl.multiple_of(half * 8, 8), 8)
        rows = pl.ds(pl.multiple_of(half * 64, 64), 64)

        def row_of(y):
            return conf[rows, y * DEPTH : (y + 1) * DEPTH].astype(F32)

        def tile(ref, *index):
            return ref[(src,) + index].astype(F32).reshape(64, DEPTH)

        edge = tile(above) * live
        for y in range(ROWS):
            cols = slice(y * DEPTH, (y + 1) * DEPTH)
            more = slice(full + y * DEPTH, full + (y + 1) * DEPTH)
            centre = row_of(y)
            if y < ROWS // 2:
                beside, live_there = tile(ahead, y) * live_next, live_next
            else:
                beside, live_there = tile(behind, y - ROWS // 2) * live_prev, live_prev
            around = lane_neighbours(centre, lane) + beside * live
            around = around + (row_of(y + 1) if y < ROWS - 1 else edge)
            if y > 0:
                around = around + row_of(y - 1)
            applied = (3.0 + pot[y : y + 1, :]) * centre - 0.5 * around
            left[rows, cols] = centre.astype(BF16)
            left[rows, more] = beside.astype(BF16)
            right[rows, cols] = applied.astype(BF16)
            right[rows, more] = (centre * (-0.5 * live_there)).astype(BF16)
        last = slice(2 * full, 2 * full + DEPTH)
        left[rows, last] = edge.astype(BF16)
        right[rows, last] = (row_of(ROWS - 1) * -0.5).astype(BF16)

    gram_blocks(left, right, gram)
    split_rows(pairs, gram, core, mine, theirs)


VMEM = pl.BlockSpec(memory_space=pltpu.VMEM)
SMEM = pl.BlockSpec(memory_space=pltpu.SMEM)
SHARE = jax.ShapeDtypeStruct((XD, YD, 8, ZD, W), F32)
CELLS = ROWS * DEPTH


def overlap_products(pair_flat, support_flat, where, own):
    return pl.pallas_call(
        overlap_kernel,
        out_shape=(jax.ShapeDtypeStruct((NB * W, CELLS), BF16), SHARE, SHARE),
        in_specs=[SMEM] * 3 + [VMEM],
        out_specs=(VMEM,) * 3,
        scratch_shapes=[pltpu.VMEM((NB, NB * W, W), F32)],
        compiler_params=pltpu.CompilerParams(vmem_limit_bytes=16 << 20),
        name="overlap_products",
    )(pair_flat, support_flat, where, own)


def hamiltonian_products(pair_flat, support_flat, where, conf, ahead, behind, above, pot):
    return pl.pallas_call(
        hamiltonian_kernel,
        out_shape=(SHARE, SHARE),
        in_specs=[SMEM] * 3 + [VMEM] * 5,
        out_specs=(VMEM,) * 2,
        scratch_shapes=[
            pltpu.VMEM((NB * W, 2 * CELLS + DEPTH), BF16),
            pltpu.VMEM((NB * W, 2 * CELLS + DEPTH), BF16),
            pltpu.VMEM((NB, NB * W, W), F32),
        ],
        compiler_params=pltpu.CompilerParams(vmem_limit_bytes=26 << 20),
        name="hamiltonian_products",
    )(pair_flat, support_flat, where, conf, ahead, behind, above, pot)


def orbital_kernel(support, where, phi, below, above, pot_low, pot_mid, pot_high, out, pot):
    block, row_z = where[2], where[0] // 8
    core = where[1]
    for step, piece in enumerate((pot_low, pot_mid, pot_high)):
        pot[step] = piece[...]
    lane = lax.broadcasted_iota(jnp.int32, (8, ROWS, DEPTH), 2)
    row = lax.broadcasted_iota(jnp.int32, (8, ROWS, DEPTH), 1)

    def masked(x):
        return phi[:, x].astype(F32) * flag(support, block, x)

    def step(x, carry):
        before, _ = carry
        centre = phi[:, x].astype(F32)
        after = masked(lax.rem(x + 1, PLANES))
        low = jnp.where(row == 0, below[:, x].astype(F32), pltpu.roll(centre, 1, 1))
        high = jnp.where(row == ROWS - 1, above[:, x].astype(F32), pltpu.roll(centre, ROWS - 1, 1))
        around = lane_neighbours(centre, lane) + low + high + before + after
        live = flag(support, block, x)
        ahead_by = lax.rem(x // 8 - row_z + ZD, ZD) + 1
        values = pot[lax.rem(ahead_by, 3), lax.rem(x + core, CD), ahead_by // 3, lax.rem(x // 2, XD)]
        applied = ((3.0 + values)[None] * centre - 0.5 * around) * live
        out[:, x] = applied.astype(BF16)
        return centre * live, 0

    lax.fori_loop(0, PLANES, step, (masked(PLANES - 1), 0))


def orbital_apply(support_flat, where, phi, below, above, pieces):
    return pl.pallas_call(
        orbital_kernel,
        out_shape=jax.ShapeDtypeStruct(phi.shape, BF16),
        in_specs=[SMEM] * 2 + [VMEM] * 6,
        out_specs=VMEM,
        scratch_shapes=[pltpu.VMEM((3, CD, len(STRIDE), XD, ROWS, DEPTH), F32)],
        compiler_params=pltpu.CompilerParams(vmem_limit_bytes=14 << 20),
        name="orbital_apply",
    )(support_flat, where, phi, below, above, *pieces)


def ring(count, shift):
    return [(i, (i + shift) % count) for i in range(count)]


def local(phi, potential, pair_list, support):
    region = lax.axis_index(REGION)
    core = lax.axis_index("c")
    where = jnp.stack([region, core, region // 16]).astype(jnp.int32)
    pair_flat = pair_list.reshape(-1)
    support_flat = support.reshape(-1)

    own = lax.all_to_all(phi.transpose(1, 2, 0, 3), REGION, split_axis=0, concat_axis=0, tiled=True)

    planes = lax.all_gather(potential, "x", axis=0, tiled=True)
    row_below = lax.ppermute(phi[:, :, 7:], "y", ring(YD, 1))
    row_above = lax.ppermute(phi[:, :, :1], "y", ring(YD, -1))
    planes, row_below, row_above = lax.optimization_barrier((planes, row_below, row_above))
    strided = [lax.ppermute(planes, "z", ring(ZD, -s)) if s else planes for s in STRIDE]
    own, strided = lax.optimization_barrier((own, strided))

    own, low_half, high_half, edge = lax.optimization_barrier((own, own[:, :4], own[:, 4:], own[:, 0]))
    ahead = lax.ppermute(low_half, REGION, ring(PLANES, -1))
    behind = lax.ppermute(high_half, REGION, ring(PLANES, 1))
    above = lax.ppermute(edge, "y", ring(YD, -1))
    own, above = lax.optimization_barrier((own, above))
    conf, mine_s, theirs_s = overlap_products(pair_flat, support_flat, where, own)
    swap = [(0, 1), (1, 0)]
    total_s = mine_s + lax.ppermute(theirs_s, "c", swap)
    mine_h, theirs_h = hamiltonian_products(pair_flat, support_flat, where, conf, ahead, behind, above,
                                            potential[0])
    total_h = mine_h + lax.ppermute(theirs_h, "c", swap)
    total = jnp.stack([total_s, total_h], axis=2).reshape(XD * YD, 2, 8, ZD, W).astype(BF16)
    total, strided = lax.optimization_barrier((total, strided))
    column = jnp.stack(strided)
    column = jnp.stack([column, lax.ppermute(column, "c", swap)])
    pieces = [lax.ppermute(column, "z", ring(ZD, 1)), column, lax.ppermute(column, "z", ring(ZD, -1))]
    shares = lax.all_to_all(total, ("x", "y"), split_axis=0, concat_axis=0, tiled=True)
    partial = jnp.sum(shares.astype(F32), axis=0).transpose(2, 0, 1, 3)
    partial, pieces = lax.optimization_barrier((partial, pieces))
    hphi = orbital_apply(support_flat, where, phi, row_below, row_above, pieces)
    shares = lax.all_to_all(partial, ("z",), split_axis=0, concat_axis=0, tiled=True)
    result = jnp.sum(shares, axis=0)
    return result[0], result[1], hphi


def solution(mesh):
    fine = Mesh(mesh.devices.reshape(ZD, XD, CD, YD), ("z", "x", "c", "y"))
    in_specs = (P(REGION, None, "y", None), P(REGION, "y", None), P(), P())
    out_specs = (P("y", REGION), P("y", REGION), P(REGION, None, "y", None))
    return jax.shard_map(local, mesh=fine, in_specs=in_specs, out_specs=out_specs, check_vma=False)
```

```python
import functools

import jax
import jax.numpy as jnp
from jax import lax
from jax.experimental import pallas as pl
from jax.experimental.pallas import tpu as pltpu
from jax.sharding import Mesh, PartitionSpec as P

W = 128
NB = 8
ROWS = 8
DEPTH = 128
PLANES = 128
PAIRS = 32
ZD, XD, CD, YD = 16, 4, 2, 4
REGION = ("z", "x", "c")
STRIDE = (0, 3, 6, 9, 12, 15)
F32 = jnp.float32
BF16 = jnp.bfloat16


def flag(support, block, plane):
    return (support[block * PLANES + plane] > 0).astype(F32)


def lane_neighbours(tile, lane):
    axis = tile.ndim - 1
    low = jnp.where(lane == 0, 0.0, pltpu.roll(tile, 1, axis))
    high = jnp.where(lane == DEPTH - 1, 0.0, pltpu.roll(tile, DEPTH - 1, axis))
    return low + high


def split_rows(pairs, gram, core, mine, theirs):
    @pl.loop(0, PAIRS)
    def _(k):
        i, j = pairs[2 * k], pairs[2 * k + 1]
        group, member = k // 8, lax.rem(k, 8)
        for x in range(XD):
            mine[x, group, member] = gram[j, pl.ds(i * W + 2 * x + core, ZD, stride=8), :]
            theirs[x, group, member] = gram[j, pl.ds(i * W + 2 * x + 1 - core, ZD, stride=8), :]


def gram_blocks(left, right, gram):
    @pl.loop(0, NB // 4)
    def _(n):
        cols = pl.ds(pl.multiple_of(n * 4 * W, 4 * W), 4 * W)
        product = lax.dot_general(left[...], right[cols, :], (((1,), (1,)), ((), ())),
                                  preferred_element_type=F32)
        for part in range(4):
            gram[4 * n + part] = product[:, part * W : (part + 1) * W]


def overlap_kernel(pairs, support, where, own, conf, mine, theirs, gram):
    plane, core = where[0], where[1]

    @pl.loop(0, NB)
    def _(block):
        live = flag(support, block, plane)
        for y in range(ROWS):
            tile = own[pl.ds(block * 16, 16), y].astype(F32).reshape(W, DEPTH) * live
            conf[pl.ds(pl.multiple_of(block * W, W), W), y * DEPTH : (y + 1) * DEPTH] = tile.astype(BF16)

    gram_blocks(conf, conf, gram)
    split_rows(pairs, gram, core, mine, theirs)


def hamiltonian_kernel(pairs, support, where, conf, ahead, behind, above, pot,
                       mine, theirs, left, right, gram):
    plane, core = where[0], where[1]
    nxt = lax.rem(plane + 1, PLANES)
    prv = lax.rem(plane + PLANES - 1, PLANES)
    lane = lax.broadcasted_iota(jnp.int32, (64, DEPTH), 1)
    full = ROWS * DEPTH

    @pl.loop(0, 2 * NB)
    def _(half):
        block = half // 2
        live = flag(support, block, plane)
        live_next = flag(support, block, nxt)
        live_prev = flag(support, block, prv)
        src = pl.ds(pl.multiple_of(half * 8, 8), 8)
        rows = pl.ds(pl.multiple_of(half * 64, 64), 64)

        def row_of(y):
            return conf[rows, y * DEPTH : (y + 1) * DEPTH].astype(F32)

        def tile(ref, *index):
            return ref[(src,) + index].astype(F32).reshape(64, DEPTH)

        edge = tile(above) * live
        for y in range(ROWS):
            cols = slice(y * DEPTH, (y + 1) * DEPTH)
            more = slice(full + y * DEPTH, full + (y + 1) * DEPTH)
            centre = row_of(y)
            if y < ROWS // 2:
                beside, live_there = tile(ahead, y) * live_next, live_next
            else:
                beside, live_there = tile(behind, y - ROWS // 2) * live_prev, live_prev
            around = lane_neighbours(centre, lane) + beside * live
            around = around + (row_of(y + 1) if y < ROWS - 1 else edge)
            if y > 0:
                around = around + row_of(y - 1)
            applied = (3.0 + pot[y : y + 1, :]) * centre - 0.5 * around
            left[rows, cols] = centre.astype(BF16)
            left[rows, more] = beside.astype(BF16)
            right[rows, cols] = applied.astype(BF16)
            right[rows, more] = (centre * (-0.5 * live_there)).astype(BF16)
        last = slice(2 * full, 2 * full + DEPTH)
        left[rows, last] = edge.astype(BF16)
        right[rows, last] = (row_of(ROWS - 1) * -0.5).astype(BF16)

    gram_blocks(left, right, gram)
    split_rows(pairs, gram, core, mine, theirs)


VMEM = pl.BlockSpec(memory_space=pltpu.VMEM)
SMEM = pl.BlockSpec(memory_space=pltpu.SMEM)
SHARE = jax.ShapeDtypeStruct((XD, YD, 8, ZD, W), F32)
CELLS = ROWS * DEPTH


def overlap_products(pair_flat, support_flat, where, own):
    return pl.pallas_call(
        overlap_kernel,
        out_shape=(jax.ShapeDtypeStruct((NB * W, CELLS), BF16), SHARE, SHARE),
        in_specs=[SMEM] * 3 + [VMEM],
        out_specs=(VMEM,) * 3,
        scratch_shapes=[pltpu.VMEM((NB, NB * W, W), F32)],
        compiler_params=pltpu.CompilerParams(vmem_limit_bytes=16 << 20),
        cost_estimate=pl.CostEstimate(flops=2 * 10**9, transcendentals=0, bytes_accessed=8 << 20),
        name="overlap_products",
    )(pair_flat, support_flat, where, own)


def hamiltonian_products(pair_flat, support_flat, where, conf, ahead, behind, above, pot):
    return pl.pallas_call(
        hamiltonian_kernel,
        out_shape=(SHARE, SHARE),
        in_specs=[SMEM] * 3 + [VMEM] * 5,
        out_specs=(VMEM,) * 2,
        scratch_shapes=[
            pltpu.VMEM((NB * W, 2 * CELLS + DEPTH), BF16),
            pltpu.VMEM((NB * W, 2 * CELLS + DEPTH), BF16),
            pltpu.VMEM((NB, NB * W, W), F32),
        ],
        compiler_params=pltpu.CompilerParams(vmem_limit_bytes=26 << 20),
        cost_estimate=pl.CostEstimate(flops=5 * 10**9, transcendentals=0, bytes_accessed=8 << 20),
        name="hamiltonian_products",
    )(pair_flat, support_flat, where, conf, ahead, behind, above, pot)


def orbital_kernel(support, where, phi, below, above, pot_low, pot_mid, pot_high, out, pot):
    block, row_z = where[2], where[0] // 8
    core = where[1]
    for step, piece in enumerate((pot_low, pot_mid, pot_high)):
        pot[step] = piece[...]
    lane = lax.broadcasted_iota(jnp.int32, (8, ROWS, DEPTH), 2)
    row = lax.broadcasted_iota(jnp.int32, (8, ROWS, DEPTH), 1)

    def masked(x):
        return phi[:, x].astype(F32) * flag(support, block, x)

    def step(x, carry):
        before, _ = carry
        centre = phi[:, x].astype(F32)
        after = masked(lax.rem(x + 1, PLANES))
        low = jnp.where(row == 0, below[:, x].astype(F32), pltpu.roll(centre, 1, 1))
        high = jnp.where(row == ROWS - 1, above[:, x].astype(F32), pltpu.roll(centre, ROWS - 1, 1))
        around = lane_neighbours(centre, lane) + low + high + before + after
        live = flag(support, block, x)
        ahead_by = lax.rem(x // 8 - row_z + ZD, ZD) + 1
        values = pot[lax.rem(ahead_by, 3), lax.rem(x + core, CD), ahead_by // 3, lax.rem(x // 2, XD)]
        applied = ((3.0 + values)[None] * centre - 0.5 * around) * live
        out[:, x] = applied.astype(BF16)
        return centre * live, 0

    lax.fori_loop(0, PLANES, step, (masked(PLANES - 1), 0))


def orbital_apply(support_flat, where, phi, below, above, pieces):
    return pl.pallas_call(
        orbital_kernel,
        out_shape=jax.ShapeDtypeStruct(phi.shape, BF16),
        in_specs=[SMEM] * 2 + [VMEM] * 6,
        out_specs=VMEM,
        scratch_shapes=[pltpu.VMEM((3, CD, len(STRIDE), XD, ROWS, DEPTH), F32)],
        compiler_params=pltpu.CompilerParams(vmem_limit_bytes=14 << 20),
        name="orbital_apply",
    )(support_flat, where, phi, below, above, *pieces)


def ring(count, shift):
    return [(i, (i + shift) % count) for i in range(count)]


def local(phi, potential, pair_list, support):
    region = lax.axis_index(REGION)
    core = lax.axis_index("c")
    where = jnp.stack([region, core, region // 16]).astype(jnp.int32)
    pair_flat = pair_list.reshape(-1)
    support_flat = support.reshape(-1)

    own = lax.all_to_all(phi.transpose(1, 2, 0, 3), REGION, split_axis=0, concat_axis=0, tiled=True)

    planes = lax.all_gather(potential, "x", axis=0, tiled=True)
    row_below = lax.ppermute(phi[:, :, 7:], "y", ring(YD, 1))
    row_above = lax.ppermute(phi[:, :, :1], "y", ring(YD, -1))
    planes, row_below, row_above = lax.optimization_barrier((planes, row_below, row_above))
    strided = [lax.ppermute(planes, "z", ring(ZD, -s)) if s else planes for s in STRIDE]
    own, strided = lax.optimization_barrier((own, strided))

    own, low_half, high_half, edge = lax.optimization_barrier((own, own[:, :4], own[:, 4:], own[:, 0]))
    ahead = lax.ppermute(low_half, REGION, ring(PLANES, -1))
    behind = lax.ppermute(high_half, REGION, ring(PLANES, 1))
    above = lax.ppermute(edge, "y", ring(YD, -1))
    conf, mine_s, theirs_s = overlap_products(pair_flat, support_flat, where, own)
    swap = [(0, 1), (1, 0)]
    total_s = mine_s + lax.ppermute(theirs_s, "c", swap)
    mine_h, theirs_h = hamiltonian_products(pair_flat, support_flat, where, conf, ahead, behind, above,
                                            potential[0])
    total_h = mine_h + lax.ppermute(theirs_h, "c", swap)
    total = jnp.stack([total_s, total_h], axis=2).reshape(XD * YD, 2, 8, ZD, W).astype(BF16)
    total, strided = lax.optimization_barrier((total, strided))
    column = jnp.stack(strided)
    column = jnp.stack([column, lax.ppermute(column, "c", swap)])
    pieces = [lax.ppermute(column, "z", ring(ZD, 1)), column, lax.ppermute(column, "z", ring(ZD, -1))]
    shares = lax.all_to_all(total, ("x", "y"), split_axis=0, concat_axis=0, tiled=True)
    partial = jnp.sum(shares.astype(F32), axis=0).transpose(2, 0, 1, 3)
    partial, pieces = lax.optimization_barrier((partial, pieces))
    hphi = orbital_apply(support_flat, where, phi, row_below, row_above, pieces)
    shares = lax.all_to_all(partial, ("z",), split_axis=0, concat_axis=0, tiled=True)
    result = jnp.sum(shares, axis=0)
    return result[0], result[1], hphi


def solution(mesh):
    fine = Mesh(mesh.devices.reshape(ZD, XD, CD, YD), ("z", "x", "c", "y"))
    in_specs = (P(REGION, None, "y", None), P(REGION, "y", None), P(), P())
    out_specs = (P("y", REGION), P("y", REGION), P(REGION, None, "y", None))
    return jax.shard_map(local, mesh=fine, in_specs=in_specs, out_specs=out_specs, check_vma=False)
```

```python
import functools

import jax
import jax.numpy as jnp
from jax import lax
from jax.experimental import pallas as pl
from jax.experimental.pallas import tpu as pltpu
from jax.sharding import Mesh, PartitionSpec as P

W = 128
NB = 8
ROWS = 8
DEPTH = 128
PLANES = 128
PAIRS = 32
ZD, XD, CD, YD = 16, 4, 2, 4
REGION = ("z", "x", "c")
STRIDE = (0, 4, 8, 12)
SHIFTS = (-1, 0, 1, 2)
F32 = jnp.float32
BF16 = jnp.bfloat16


def flag(support, block, plane):
    return (support[block * PLANES + plane] > 0).astype(F32)


def lane_neighbours(tile, lane):
    axis = tile.ndim - 1
    low = jnp.where(lane == 0, 0.0, pltpu.roll(tile, 1, axis))
    high = jnp.where(lane == DEPTH - 1, 0.0, pltpu.roll(tile, DEPTH - 1, axis))
    return low + high


def split_rows(pairs, gram, core, mine, theirs):
    @pl.loop(0, PAIRS)
    def _(k):
        i, j = pairs[2 * k], pairs[2 * k + 1]
        group, member = k // 8, lax.rem(k, 8)
        for x in range(XD):
            mine[x, group, member] = gram[j, pl.ds(i * W + 2 * x + core, ZD, stride=8), :]
            theirs[x, group, member] = gram[j, pl.ds(i * W + 2 * x + 1 - core, ZD, stride=8), :]


def gram_blocks(left, right, gram):
    @pl.loop(0, NB // 4)
    def _(n):
        cols = pl.ds(pl.multiple_of(n * 4 * W, 4 * W), 4 * W)
        product = lax.dot_general(left[...], right[cols, :], (((1,), (1,)), ((), ())),
                                  preferred_element_type=F32)
        for part in range(4):
            gram[4 * n + part] = product[:, part * W : (part + 1) * W]


def overlap_kernel(pairs, support, where, own, conf, mine, theirs, gram):
    plane, core = where[0], where[1]

    @pl.loop(0, NB)
    def _(block):
        live = flag(support, block, plane)
        for y in range(ROWS):
            tile = own[pl.ds(block * 16, 16), y].astype(F32).reshape(W, DEPTH) * live
            conf[pl.ds(pl.multiple_of(block * W, W), W), y * DEPTH : (y + 1) * DEPTH] = tile.astype(BF16)

    gram_blocks(conf, conf, gram)
    split_rows(pairs, gram, core, mine, theirs)


def hamiltonian_kernel(pairs, support, where, conf, ahead, behind, above, pot,
                       mine, theirs, left, right, gram):
    plane, core = where[0], where[1]
    nxt = lax.rem(plane + 1, PLANES)
    prv = lax.rem(plane + PLANES - 1, PLANES)
    lane = lax.broadcasted_iota(jnp.int32, (64, DEPTH), 1)
    full = ROWS * DEPTH

    @pl.loop(0, 2 * NB)
    def _(half):
        block = half // 2
        live = flag(support, block, plane)
        live_next = flag(support, block, nxt)
        live_prev = flag(support, block, prv)
        src = pl.ds(pl.multiple_of(half * 8, 8), 8)
        rows = pl.ds(pl.multiple_of(half * 64, 64), 64)

        def row_of(y):
            return conf[rows, y * DEPTH : (y + 1) * DEPTH].astype(F32)

        def tile(ref, *index):
            return ref[(src,) + index].astype(F32).reshape(64, DEPTH)

        edge = tile(above) * live
        for y in range(ROWS):
            cols = slice(y * DEPTH, (y + 1) * DEPTH)
            more = slice(full + y * DEPTH, full + (y + 1) * DEPTH)
            centre = row_of(y)
            if y < ROWS // 2:
                beside, live_there = tile(ahead, y) * live_next, live_next
            else:
                beside, live_there = tile(behind, y - ROWS // 2) * live_prev, live_prev
            around = lane_neighbours(centre, lane) + beside * live
            around = around + (row_of(y + 1) if y < ROWS - 1 else edge)
            if y > 0:
                around = around + row_of(y - 1)
            applied = (3.0 + pot[y : y + 1, :]) * centre - 0.5 * around
            left[rows, cols] = centre.astype(BF16)
            left[rows, more] = beside.astype(BF16)
            right[rows, cols] = applied.astype(BF16)
            right[rows, more] = (centre * (-0.5 * live_there)).astype(BF16)
        last = slice(2 * full, 2 * full + DEPTH)
        left[rows, last] = edge.astype(BF16)
        right[rows, last] = (row_of(ROWS - 1) * -0.5).astype(BF16)

    gram_blocks(left, right, gram)
    split_rows(pairs, gram, core, mine, theirs)


VMEM = pl.BlockSpec(memory_space=pltpu.VMEM)
SMEM = pl.BlockSpec(memory_space=pltpu.SMEM)
SHARE = jax.ShapeDtypeStruct((XD, YD, 8, ZD, W), F32)
CELLS = ROWS * DEPTH


def overlap_products(pair_flat, support_flat, where, own):
    return pl.pallas_call(
        overlap_kernel,
        out_shape=(jax.ShapeDtypeStruct((NB * W, CELLS), BF16), SHARE, SHARE),
        in_specs=[SMEM] * 3 + [VMEM],
        out_specs=(VMEM,) * 3,
        scratch_shapes=[pltpu.VMEM((NB, NB * W, W), F32)],
        compiler_params=pltpu.CompilerParams(vmem_limit_bytes=16 << 20),
        cost_estimate=pl.CostEstimate(flops=2 * 10**9, transcendentals=0, bytes_accessed=8 << 20),
        name="overlap_products",
    )(pair_flat, support_flat, where, own)


def hamiltonian_products(pair_flat, support_flat, where, conf, ahead, behind, above, pot):
    return pl.pallas_call(
        hamiltonian_kernel,
        out_shape=(SHARE, SHARE),
        in_specs=[SMEM] * 3 + [VMEM] * 5,
        out_specs=(VMEM,) * 2,
        scratch_shapes=[
            pltpu.VMEM((NB * W, 2 * CELLS + DEPTH), BF16),
            pltpu.VMEM((NB * W, 2 * CELLS + DEPTH), BF16),
            pltpu.VMEM((NB, NB * W, W), F32),
        ],
        compiler_params=pltpu.CompilerParams(vmem_limit_bytes=26 << 20),
        cost_estimate=pl.CostEstimate(flops=5 * 10**9, transcendentals=0, bytes_accessed=8 << 20),
        name="hamiltonian_products",
    )(pair_flat, support_flat, where, conf, ahead, behind, above, pot)


def orbital_kernel(support, where, phi, below, above, pot_0, pot_1, pot_2, pot_3, out, pot):
    block, row_z = where[2], where[0] // 8
    core = where[1]
    for step, piece in enumerate((pot_0, pot_1, pot_2, pot_3)):
        pot[step] = piece[...]
    lane = lax.broadcasted_iota(jnp.int32, (8, ROWS, DEPTH), 2)
    row = lax.broadcasted_iota(jnp.int32, (8, ROWS, DEPTH), 1)

    def masked(x):
        return phi[:, x].astype(F32) * flag(support, block, x)

    def step(x, carry):
        before, _ = carry
        centre = phi[:, x].astype(F32)
        after = masked(lax.rem(x + 1, PLANES))
        low = jnp.where(row == 0, below[:, x].astype(F32), pltpu.roll(centre, 1, 1))
        high = jnp.where(row == ROWS - 1, above[:, x].astype(F32), pltpu.roll(centre, ROWS - 1, 1))
        around = lane_neighbours(centre, lane) + low + high + before + after
        live = flag(support, block, x)
        ahead_by = lax.rem(x // 8 - row_z + ZD + 1, ZD)
        values = pot[lax.rem(ahead_by, 4), lax.rem(x + core, CD), ahead_by // 4, lax.rem(x // 2, XD)]
        applied = ((3.0 + values)[None] * centre - 0.5 * around) * live
        out[:, x] = applied.astype(BF16)
        return centre * live, 0

    lax.fori_loop(0, PLANES, step, (masked(PLANES - 1), 0))


def orbital_apply(support_flat, where, phi, below, above, pieces):
    return pl.pallas_call(
        orbital_kernel,
        out_shape=jax.ShapeDtypeStruct(phi.shape, BF16),
        in_specs=[SMEM] * 2 + [VMEM] * 7,
        out_specs=VMEM,
        scratch_shapes=[pltpu.VMEM((len(SHIFTS), CD, len(STRIDE), XD, ROWS, DEPTH), F32)],
        compiler_params=pltpu.CompilerParams(vmem_limit_bytes=14 << 20),
        name="orbital_apply",
    )(support_flat, where, phi, below, above, *pieces)


def ring(count, shift):
    return [(i, (i + shift) % count) for i in range(count)]


def local(phi, potential, pair_list, support):
    region = lax.axis_index(REGION)
    core = lax.axis_index("c")
    where = jnp.stack([region, core, region // 16]).astype(jnp.int32)
    pair_flat = pair_list.reshape(-1)
    support_flat = support.reshape(-1)

    own = lax.all_to_all(phi.transpose(1, 2, 0, 3), REGION, split_axis=0, concat_axis=0, tiled=True)

    planes = lax.all_gather(potential, "x", axis=0, tiled=True)
    row_below = lax.ppermute(phi[:, :, 7:], "y", ring(YD, 1))
    row_above = lax.ppermute(phi[:, :, :1], "y", ring(YD, -1))
    planes, row_below, row_above = lax.optimization_barrier((planes, row_below, row_above))
    strided = [lax.ppermute(planes, "z", ring(ZD, -s)) if s else planes for s in STRIDE]
    own, strided = lax.optimization_barrier((own, strided))

    own, low_half, high_half, edge = lax.optimization_barrier((own, own[:, :4], own[:, 4:], own[:, 0]))
    ahead = lax.ppermute(low_half, REGION, ring(PLANES, -1))
    behind = lax.ppermute(high_half, REGION, ring(PLANES, 1))
    above = lax.ppermute(edge, "y", ring(YD, -1))
    conf, mine_s, theirs_s = overlap_products(pair_flat, support_flat, where, own)
    swap = [(0, 1), (1, 0)]
    total_s = mine_s + lax.ppermute(theirs_s, "c", swap)
    mine_h, theirs_h = hamiltonian_products(pair_flat, support_flat, where, conf, ahead, behind, above,
                                            potential[0])
    total_h = mine_h + lax.ppermute(theirs_h, "c", swap)
    total = jnp.stack([total_s, total_h], axis=2).reshape(XD * YD, 2, 8, ZD, W).astype(BF16)
    total, strided = lax.optimization_barrier((total, strided))
    column = jnp.stack(strided)
    column = jnp.stack([column, lax.ppermute(column, "c", swap)])
    pieces = [lax.ppermute(column, "z", ring(ZD, -s)) if s else column for s in SHIFTS]
    shares = lax.all_to_all(total, ("x", "y"), split_axis=0, concat_axis=0, tiled=True)
    partial = jnp.sum(shares.astype(F32), axis=0).transpose(2, 0, 1, 3)
    partial, pieces = lax.optimization_barrier((partial, pieces))
    hphi = orbital_apply(support_flat, where, phi, row_below, row_above, pieces)
    shares = lax.all_to_all(partial, ("z",), split_axis=0, concat_axis=0, tiled=True)
    result = jnp.sum(shares, axis=0)
    return result[0], result[1], hphi


def solution(mesh):
    fine = Mesh(mesh.devices.reshape(ZD, XD, CD, YD), ("z", "x", "c", "y"))
    in_specs = (P(REGION, None, "y", None), P(REGION, "y", None), P(), P())
    out_specs = (P("y", REGION), P("y", REGION), P(REGION, None, "y", None))
    return jax.shard_map(local, mesh=fine, in_specs=in_specs, out_specs=out_specs, check_vma=False)
```

```python
import functools

import jax
import jax.numpy as jnp
from jax import lax
from jax.experimental import pallas as pl
from jax.experimental.pallas import tpu as pltpu
from jax.sharding import Mesh, PartitionSpec as P

W = 128
NB = 8
ROWS = 8
DEPTH = 128
PLANES = 128
PAIRS = 32
ZD, XD, CD, YD = 16, 4, 2, 4
REGION = ("z", "x", "c")
STRIDE = (0, 4, 8, 12)
SHIFTS = (-1, 0, 1, 2)
F32 = jnp.float32
BF16 = jnp.bfloat16


def flag(support, block, plane):
    return (support[block * PLANES + plane] > 0).astype(F32)


def lane_neighbours(tile, lane):
    axis = tile.ndim - 1
    low = jnp.where(lane == 0, 0.0, pltpu.roll(tile, 1, axis))
    high = jnp.where(lane == DEPTH - 1, 0.0, pltpu.roll(tile, DEPTH - 1, axis))
    return low + high


def split_rows(pairs, gram, core, mine, theirs):
    @pl.loop(0, PAIRS)
    def _(k):
        i, j = pairs[2 * k], pairs[2 * k + 1]
        group, member = k // 8, lax.rem(k, 8)
        for x in range(XD):
            mine[x, group, member] = gram[j, pl.ds(i * W + 2 * x + core, ZD, stride=8), :]
            theirs[x, group, member] = gram[j, pl.ds(i * W + 2 * x + 1 - core, ZD, stride=8), :]


def gram_blocks(left, right, gram):
    @pl.loop(0, NB // 4)
    def _(n):
        cols = pl.ds(pl.multiple_of(n * 4 * W, 4 * W), 4 * W)
        product = lax.dot_general(left[...], right[cols, :], (((1,), (1,)), ((), ())),
                                  preferred_element_type=F32)
        for part in range(4):
            gram[4 * n + part] = product[:, part * W : (part + 1) * W]


def overlap_kernel(pairs, support, where, own, conf, mine, theirs, gram):
    plane, core = where[0], where[1]

    @pl.loop(0, NB)
    def _(block):
        live = flag(support, block, plane)
        for y in range(ROWS):
            tile = own[pl.ds(block * 16, 16), y].astype(F32).reshape(W, DEPTH) * live
            conf[pl.ds(pl.multiple_of(block * W, W), W), y * DEPTH : (y + 1) * DEPTH] = tile.astype(BF16)

    gram_blocks(conf, conf, gram)
    split_rows(pairs, gram, core, mine, theirs)


def hamiltonian_kernel(pairs, support, where, conf, ahead, behind, above, pot,
                       mine, theirs, left, right, gram):
    plane, core = where[0], where[1]
    nxt = lax.rem(plane + 1, PLANES)
    prv = lax.rem(plane + PLANES - 1, PLANES)
    lane = lax.broadcasted_iota(jnp.int32, (64, DEPTH), 1)
    full = ROWS * DEPTH

    @pl.loop(0, 2 * NB)
    def _(half):
        block = half // 2
        live = flag(support, block, plane)
        live_next = flag(support, block, nxt)
        live_prev = flag(support, block, prv)
        src = pl.ds(pl.multiple_of(half * 8, 8), 8)
        rows = pl.ds(pl.multiple_of(half * 64, 64), 64)

        def row_of(y):
            return conf[rows, y * DEPTH : (y + 1) * DEPTH].astype(F32)

        def tile(ref, *index):
            return ref[(src,) + index].astype(F32).reshape(64, DEPTH)

        edge = tile(above) * live
        for y in range(ROWS):
            cols = slice(y * DEPTH, (y + 1) * DEPTH)
            more = slice(full + y * DEPTH, full + (y + 1) * DEPTH)
            centre = row_of(y)
            if y < ROWS // 2:
                beside, live_there = tile(ahead, y) * live_next, live_next
            else:
                beside, live_there = tile(behind, y - ROWS // 2) * live_prev, live_prev
            around = lane_neighbours(centre, lane) + beside * live
            around = around + (row_of(y + 1) if y < ROWS - 1 else edge)
            if y > 0:
                around = around + row_of(y - 1)
            applied = (3.0 + pot[y : y + 1, :]) * centre - 0.5 * around
            left[rows, cols] = centre.astype(BF16)
            left[rows, more] = beside.astype(BF16)
            right[rows, cols] = applied.astype(BF16)
            right[rows, more] = (centre * (-0.5 * live_there)).astype(BF16)
        last = slice(2 * full, 2 * full + DEPTH)
        left[rows, last] = edge.astype(BF16)
        right[rows, last] = (row_of(ROWS - 1) * -0.5).astype(BF16)

    gram_blocks(left, right, gram)
    split_rows(pairs, gram, core, mine, theirs)


VMEM = pl.BlockSpec(memory_space=pltpu.VMEM)
SMEM = pl.BlockSpec(memory_space=pltpu.SMEM)
SHARE = jax.ShapeDtypeStruct((XD, YD, 8, ZD, W), F32)
CELLS = ROWS * DEPTH


def overlap_products(pair_flat, support_flat, where, own):
    return pl.pallas_call(
        overlap_kernel,
        out_shape=(jax.ShapeDtypeStruct((NB * W, CELLS), BF16), SHARE, SHARE),
        in_specs=[SMEM] * 3 + [VMEM],
        out_specs=(VMEM,) * 3,
        scratch_shapes=[pltpu.VMEM((NB, NB * W, W), F32)],
        compiler_params=pltpu.CompilerParams(vmem_limit_bytes=16 << 20),
        cost_estimate=pl.CostEstimate(flops=2 * 10**9, transcendentals=0, bytes_accessed=8 << 20),
        name="overlap_products",
    )(pair_flat, support_flat, where, own)


def hamiltonian_products(pair_flat, support_flat, where, conf, ahead, behind, above, pot):
    return pl.pallas_call(
        hamiltonian_kernel,
        out_shape=(SHARE, SHARE),
        in_specs=[SMEM] * 3 + [VMEM] * 5,
        out_specs=(VMEM,) * 2,
        scratch_shapes=[
            pltpu.VMEM((NB * W, 2 * CELLS + DEPTH), BF16),
            pltpu.VMEM((NB * W, 2 * CELLS + DEPTH), BF16),
            pltpu.VMEM((NB, NB * W, W), F32),
        ],
        compiler_params=pltpu.CompilerParams(vmem_limit_bytes=26 << 20),
        cost_estimate=pl.CostEstimate(flops=5 * 10**9, transcendentals=0, bytes_accessed=8 << 20),
        name="hamiltonian_products",
    )(pair_flat, support_flat, where, conf, ahead, behind, above, pot)


def orbital_kernel(support, where, phi, below, above, pot_0, pot_1, pot_2, pot_3, out, pot):
    block, row_z = where[2], where[0] // 8
    core = where[1]
    for step, piece in enumerate((pot_0, pot_1, pot_2, pot_3)):
        pot[step] = piece[...]
    lane = lax.broadcasted_iota(jnp.int32, (8, ROWS, DEPTH), 2)
    row = lax.broadcasted_iota(jnp.int32, (8, ROWS, DEPTH), 1)

    def masked(x):
        return phi[:, x].astype(F32) * flag(support, block, x)

    def step(x, carry):
        before, _ = carry
        centre = phi[:, x].astype(F32)
        after = masked(lax.rem(x + 1, PLANES))
        low = jnp.where(row == 0, below[:, x].astype(F32), pltpu.roll(centre, 1, 1))
        high = jnp.where(row == ROWS - 1, above[:, x].astype(F32), pltpu.roll(centre, ROWS - 1, 1))
        around = lane_neighbours(centre, lane) + low + high + before + after
        live = flag(support, block, x)
        ahead_by = lax.rem(x // 8 - row_z + ZD + 1, ZD)
        values = pot[lax.rem(ahead_by, 4), lax.rem(x + core, CD), ahead_by // 4, lax.rem(x // 2, XD)]
        applied = ((3.0 + values)[None] * centre - 0.5 * around) * live
        out[:, x] = applied.astype(BF16)
        return centre * live, 0

    def eight(n, carry):
        for part in range(8):
            carry = step(8 * n + part, carry)
        return carry

    lax.fori_loop(0, PLANES // 8, eight, (masked(PLANES - 1), 0))


def orbital_apply(support_flat, where, phi, below, above, pieces):
    return pl.pallas_call(
        orbital_kernel,
        out_shape=jax.ShapeDtypeStruct(phi.shape, BF16),
        in_specs=[SMEM] * 2 + [VMEM] * 7,
        out_specs=VMEM,
        scratch_shapes=[pltpu.VMEM((len(SHIFTS), CD, len(STRIDE), XD, ROWS, DEPTH), F32)],
        compiler_params=pltpu.CompilerParams(vmem_limit_bytes=14 << 20),
        name="orbital_apply",
    )(support_flat, where, phi, below, above, *pieces)


def ring(count, shift):
    return [(i, (i + shift) % count) for i in range(count)]


def local(phi, potential, pair_list, support):
    region = lax.axis_index(REGION)
    core = lax.axis_index("c")
    where = jnp.stack([region, core, region // 16]).astype(jnp.int32)
    pair_flat = pair_list.reshape(-1)
    support_flat = support.reshape(-1)

    own = lax.all_to_all(phi.transpose(1, 2, 0, 3), REGION, split_axis=0, concat_axis=0, tiled=True)

    planes = lax.all_gather(potential, "x", axis=0, tiled=True)
    row_below = lax.ppermute(phi[:, :, 7:], "y", ring(YD, 1))
    row_above = lax.ppermute(phi[:, :, :1], "y", ring(YD, -1))
    planes, row_below, row_above = lax.optimization_barrier((planes, row_below, row_above))
    strided = [lax.ppermute(planes, "z", ring(ZD, -s)) if s else planes for s in STRIDE]
    own, strided = lax.optimization_barrier((own, strided))

    own, low_half, high_half, edge = lax.optimization_barrier((own, own[:, :4], own[:, 4:], own[:, 0]))
    ahead = lax.ppermute(low_half, REGION, ring(PLANES, -1))
    behind = lax.ppermute(high_half, REGION, ring(PLANES, 1))
    above = lax.ppermute(edge, "y", ring(YD, -1))
    conf, mine_s, theirs_s = overlap_products(pair_flat, support_flat, where, own)
    swap = [(0, 1), (1, 0)]
    total_s = mine_s + lax.ppermute(theirs_s, "c", swap)
    mine_h, theirs_h = hamiltonian_products(pair_flat, support_flat, where, conf, ahead, behind, above,
                                            potential[0])
    total_h = mine_h + lax.ppermute(theirs_h, "c", swap)
    total = jnp.stack([total_s, total_h], axis=2).reshape(XD * YD, 2, 8, ZD, W).astype(BF16)
    total, strided = lax.optimization_barrier((total, strided))
    column = jnp.stack(strided)
    column = jnp.stack([column, lax.ppermute(column, "c", swap)])
    pieces = [lax.ppermute(column, "z", ring(ZD, -s)) if s else column for s in SHIFTS]
    shares = lax.all_to_all(total, ("x", "y"), split_axis=0, concat_axis=0, tiled=True)
    partial = jnp.sum(shares.astype(F32), axis=0).transpose(2, 0, 1, 3)
    partial, pieces = lax.optimization_barrier((partial, pieces))
    hphi = orbital_apply(support_flat, where, phi, row_below, row_above, pieces)
    shares = lax.all_to_all(partial, ("z",), split_axis=0, concat_axis=0, tiled=True)
    result = jnp.sum(shares, axis=0)
    return result[0], result[1], hphi


def solution(mesh):
    fine = Mesh(mesh.devices.reshape(ZD, XD, CD, YD), ("z", "x", "c", "y"))
    in_specs = (P(REGION, None, "y", None), P(REGION, "y", None), P(), P())
    out_specs = (P("y", REGION), P("y", REGION), P(REGION, None, "y", None))
    return jax.shard_map(local, mesh=fine, in_specs=in_specs, out_specs=out_specs, check_vma=False)
```

```python
import functools

import jax
import jax.numpy as jnp
from jax import lax
from jax.experimental import pallas as pl
from jax.experimental.pallas import tpu as pltpu
from jax.sharding import Mesh, PartitionSpec as P

W = 128
NB = 8
ROWS = 8
DEPTH = 128
PLANES = 128
PAIRS = 32
ZD, XD, CD, YD = 16, 4, 2, 4
REGION = ("z", "x", "c")
STRIDE = (0, 4, 8, 12)
SHIFTS = (-1, 0, 1, 2)
F32 = jnp.float32
BF16 = jnp.bfloat16


def flag(support, block, plane):
    return (support[block * PLANES + plane] > 0).astype(F32)


def lane_neighbours(tile, lane):
    axis = tile.ndim - 1
    low = jnp.where(lane == 0, 0.0, pltpu.roll(tile, 1, axis))
    high = jnp.where(lane == DEPTH - 1, 0.0, pltpu.roll(tile, DEPTH - 1, axis))
    return low + high


def split_rows(pairs, gram, core, mine, theirs):
    @pl.loop(0, PAIRS)
    def _(k):
        i, j = pairs[2 * k], pairs[2 * k + 1]
        group, member = k // 8, lax.rem(k, 8)
        for x in range(XD):
            mine[x, group, member] = gram[j, pl.ds(i * W + 2 * x + core, ZD, stride=8), :]
            theirs[x, group, member] = gram[j, pl.ds(i * W + 2 * x + 1 - core, ZD, stride=8), :]


def gram_blocks(left, right, gram):
    @pl.loop(0, NB // 4)
    def _(n):
        cols = pl.ds(pl.multiple_of(n * 4 * W, 4 * W), 4 * W)
        product = lax.dot_general(left[...], right[cols, :], (((1,), (1,)), ((), ())),
                                  preferred_element_type=F32)
        for part in range(4):
            gram[4 * n + part] = product[:, part * W : (part + 1) * W]


def overlap_kernel(pairs, support, where, own, conf, mine, theirs, gram):
    plane, core = where[0], where[1]

    @pl.loop(0, NB)
    def _(block):
        live = flag(support, block, plane)
        for y in range(ROWS):
            tile = own[pl.ds(block * 16, 16), y].astype(F32).reshape(W, DEPTH) * live
            conf[pl.ds(pl.multiple_of(block * W, W), W), y * DEPTH : (y + 1) * DEPTH] = tile.astype(BF16)

    gram_blocks(conf, conf, gram)
    split_rows(pairs, gram, core, mine, theirs)


def hamiltonian_kernel(pairs, support, where, conf, ahead, behind, above, pot,
                       mine, theirs, left, right, gram):
    plane, core = where[0], where[1]
    nxt = lax.rem(plane + 1, PLANES)
    prv = lax.rem(plane + PLANES - 1, PLANES)
    lane = lax.broadcasted_iota(jnp.int32, (64, DEPTH), 1)
    full = ROWS * DEPTH

    @pl.loop(0, 2 * NB)
    def _(half):
        block = half // 2
        live = flag(support, block, plane)
        live_next = flag(support, block, nxt)
        live_prev = flag(support, block, prv)
        src = pl.ds(pl.multiple_of(half * 8, 8), 8)
        rows = pl.ds(pl.multiple_of(half * 64, 64), 64)

        def row_of(y):
            return conf[rows, y * DEPTH : (y + 1) * DEPTH].astype(F32)

        def tile(ref, *index):
            return ref[(src,) + index].astype(F32).reshape(64, DEPTH)

        edge = tile(above) * live
        for y in range(ROWS):
            cols = slice(y * DEPTH, (y + 1) * DEPTH)
            more = slice(full + y * DEPTH, full + (y + 1) * DEPTH)
            centre = row_of(y)
            if y < ROWS // 2:
                beside, live_there = tile(ahead, y) * live_next, live_next
            else:
                beside, live_there = tile(behind, y - ROWS // 2) * live_prev, live_prev
            around = lane_neighbours(centre, lane) + beside * live
            around = around + (row_of(y + 1) if y < ROWS - 1 else edge)
            if y > 0:
                around = around + row_of(y - 1)
            applied = (3.0 + pot[y : y + 1, :]) * centre - 0.5 * around
            left[rows, cols] = centre.astype(BF16)
            left[rows, more] = beside.astype(BF16)
            right[rows, cols] = applied.astype(BF16)
            right[rows, more] = (centre * (-0.5 * live_there)).astype(BF16)
        last = slice(2 * full, 2 * full + DEPTH)
        left[rows, last] = edge.astype(BF16)
        right[rows, last] = (row_of(ROWS - 1) * -0.5).astype(BF16)

    gram_blocks(left, right, gram)
    split_rows(pairs, gram, core, mine, theirs)


VMEM = pl.BlockSpec(memory_space=pltpu.VMEM)
SMEM = pl.BlockSpec(memory_space=pltpu.SMEM)
SHARE = jax.ShapeDtypeStruct((XD, YD, 8, ZD, W), F32)
CELLS = ROWS * DEPTH


def overlap_products(pair_flat, support_flat, where, own):
    return pl.pallas_call(
        overlap_kernel,
        out_shape=(jax.ShapeDtypeStruct((NB * W, CELLS), BF16), SHARE, SHARE),
        in_specs=[SMEM] * 3 + [VMEM],
        out_specs=(VMEM,) * 3,
        scratch_shapes=[pltpu.VMEM((NB, NB * W, W), F32)],
        compiler_params=pltpu.CompilerParams(vmem_limit_bytes=16 << 20),
        name="overlap_products",
    )(pair_flat, support_flat, where, own)


def hamiltonian_products(pair_flat, support_flat, where, conf, ahead, behind, above, pot):
    return pl.pallas_call(
        hamiltonian_kernel,
        out_shape=(SHARE, SHARE),
        in_specs=[SMEM] * 3 + [VMEM] * 5,
        out_specs=(VMEM,) * 2,
        scratch_shapes=[
            pltpu.VMEM((NB * W, 2 * CELLS + DEPTH), BF16),
            pltpu.VMEM((NB * W, 2 * CELLS + DEPTH), BF16),
            pltpu.VMEM((NB, NB * W, W), F32),
        ],
        compiler_params=pltpu.CompilerParams(vmem_limit_bytes=26 << 20),
        cost_estimate=pl.CostEstimate(flops=5 * 10**9, transcendentals=0, bytes_accessed=8 << 20),
        name="hamiltonian_products",
    )(pair_flat, support_flat, where, conf, ahead, behind, above, pot)


def orbital_kernel(support, where, phi, below, above, pot_0, pot_1, pot_2, pot_3, out, pot):
    block, row_z = where[2], where[0] // 8
    core = where[1]
    for step, piece in enumerate((pot_0, pot_1, pot_2, pot_3)):
        pot[step] = piece[...]
    lane = lax.broadcasted_iota(jnp.int32, (8, ROWS, DEPTH), 2)
    row = lax.broadcasted_iota(jnp.int32, (8, ROWS, DEPTH), 1)

    def masked(x):
        return phi[:, x].astype(F32) * flag(support, block, x)

    def step(x, carry):
        before, _ = carry
        centre = phi[:, x].astype(F32)
        after = masked(lax.rem(x + 1, PLANES))
        low = jnp.where(row == 0, below[:, x].astype(F32), pltpu.roll(centre, 1, 1))
        high = jnp.where(row == ROWS - 1, above[:, x].astype(F32), pltpu.roll(centre, ROWS - 1, 1))
        around = lane_neighbours(centre, lane) + low + high + before + after
        live = flag(support, block, x)
        ahead_by = lax.rem(x // 8 - row_z + ZD + 1, ZD)
        values = pot[lax.rem(ahead_by, 4), lax.rem(x + core, CD), ahead_by // 4, lax.rem(x // 2, XD)]
        applied = ((3.0 + values)[None] * centre - 0.5 * around) * live
        out[:, x] = applied.astype(BF16)
        return centre * live, 0

    def eight(n, carry):
        for part in range(8):
            carry = step(8 * n + part, carry)
        return carry

    lax.fori_loop(0, PLANES // 8, eight, (masked(PLANES - 1), 0))


def orbital_apply(support_flat, where, phi, below, above, pieces):
    return pl.pallas_call(
        orbital_kernel,
        out_shape=jax.ShapeDtypeStruct(phi.shape, BF16),
        in_specs=[SMEM] * 2 + [VMEM] * 7,
        out_specs=VMEM,
        scratch_shapes=[pltpu.VMEM((len(SHIFTS), CD, len(STRIDE), XD, ROWS, DEPTH), F32)],
        compiler_params=pltpu.CompilerParams(vmem_limit_bytes=14 << 20),
        name="orbital_apply",
    )(support_flat, where, phi, below, above, *pieces)


def ring(count, shift):
    return [(i, (i + shift) % count) for i in range(count)]


def local(phi, potential, pair_list, support):
    region = lax.axis_index(REGION)
    core = lax.axis_index("c")
    where = jnp.stack([region, core, region // 16]).astype(jnp.int32)
    pair_flat = pair_list.reshape(-1)
    support_flat = support.reshape(-1)

    own = lax.all_to_all(phi.transpose(1, 2, 0, 3), REGION, split_axis=0, concat_axis=0, tiled=True)

    planes = lax.all_gather(potential, "x", axis=0, tiled=True)
    row_below = lax.ppermute(phi[:, :, 7:], "y", ring(YD, 1))
    row_above = lax.ppermute(phi[:, :, :1], "y", ring(YD, -1))
    planes, row_below, row_above = lax.optimization_barrier((planes, row_below, row_above))
    strided = [lax.ppermute(planes, "z", ring(ZD, -s)) if s else planes for s in STRIDE]
    own, strided = lax.optimization_barrier((own, strided))

    own, low_half, high_half, edge = lax.optimization_barrier((own, own[:, :4], own[:, 4:], own[:, 0]))
    ahead = lax.ppermute(low_half, REGION, ring(PLANES, -1))
    behind = lax.ppermute(high_half, REGION, ring(PLANES, 1))
    above = lax.ppermute(edge, "y", ring(YD, -1))
    conf, mine_s, theirs_s = overlap_products(pair_flat, support_flat, where, own)
    swap = [(0, 1), (1, 0)]
    total_s = mine_s + lax.ppermute(theirs_s, "c", swap)
    mine_h, theirs_h = hamiltonian_products(pair_flat, support_flat, where, conf, ahead, behind, above,
                                            potential[0])
    total_h = mine_h + lax.ppermute(theirs_h, "c", swap)
    total = jnp.stack([total_s, total_h], axis=2).reshape(XD * YD, 2, 8, ZD, W).astype(BF16)
    total, strided = lax.optimization_barrier((total, strided))
    column = jnp.stack(strided)
    column = jnp.stack([column, lax.ppermute(column, "c", swap)])
    pieces = [lax.ppermute(column, "z", ring(ZD, -s)) if s else column for s in SHIFTS]
    shares = lax.all_to_all(total, ("x", "y"), split_axis=0, concat_axis=0, tiled=True)
    partial = jnp.sum(shares.astype(F32), axis=0).transpose(2, 0, 1, 3)
    partial, pieces = lax.optimization_barrier((partial, pieces))
    hphi = orbital_apply(support_flat, where, phi, row_below, row_above, pieces)
    shares = lax.all_to_all(partial, ("z",), split_axis=0, concat_axis=0, tiled=True)
    result = jnp.sum(shares, axis=0)
    return result[0], result[1], hphi


def solution(mesh):
    fine = Mesh(mesh.devices.reshape(ZD, XD, CD, YD), ("z", "x", "c", "y"))
    in_specs = (P(REGION, None, "y", None), P(REGION, "y", None), P(), P())
    out_specs = (P("y", REGION), P("y", REGION), P(REGION, None, "y", None))
    return jax.shard_map(local, mesh=fine, in_specs=in_specs, out_specs=out_specs, check_vma=False)
```
